256 devices in a mesh: lat: 16 (over x, y_hi, core), lon: 16 (over y_lo, z).
Axes of the slice: x: 4, y: 4 (y_hi: 2, y_lo: 2; y = y_hi * 2 + y_lo), z: 8, core: 2. Of those that a mesh axis runs over, the one named last changes fastest.
Arguments:
- feature: bfloat16 [512, 512, 384], P('lat', 'lon'), may hold values from -6 to 6
- coverage: int32 [512, 512], P('lat', 'lon'), may hold values 0 or 1
- band_rows: int32 [16], replicated, may hold values from 3 to 32, as said below
- depth_weight: bfloat16 [7, 7, 384], replicated, may hold values from -0.875 to 0.875
- norm_gain: float32 [384], replicated, may hold values from 0.25 to 1.75
- norm_shift: float32 [384], replicated, may hold values from -3 to 3
- up_weight: bfloat16 [384, 1536], P('lon'), may hold values from -0.3125 to 0.3125
- up_bias: float32 [1536], replicated, may hold values from -3 to 3
- down_weight: bfloat16 [1536, 384], P('lon'), may hold values from -0.15625 to 0.15625
- down_bias: float32 [384], replicated, may hold values from -3 to 3
- layer_scale: float32 [384], replicated, may hold values from 0.3 to 1.5
- cotangent: bfloat16 [512, 512, 384], P('lat', 'lon'), may hold values from -6 to 6
Outputs:
- block_out: bfloat16 [512, 512, 384], P('lat', 'lon')
- grad_in: bfloat16 [512, 512, 384], P('lat', 'lon')
- grad_up: float32 [384, 1536], P('lon')
- grad_down: float32 [1536, 384], P('lon')
- grad_depth: float32 [7, 7, 384], replicated
The draws below stay inside these ranges and needn't reach their ends.
Inputs may be any that keep to these rules, and one draw needn't show every extreme that they name: `band_rows`: every band has 3 or more rows, the bands' rows sum to 256, and one band has exactly 32.
All inputs are finite; a program needn't handle non-finite values. No bound on the sum of `coverage` on one device may be relied on, other than what follows from the above.
Results may differ from the reference program's by a relative error of at most 0.0066.
Values may be sent and summed in bfloat16 or wider, within the bound.
A program may use at most 64 MiB of HBM per device.

```python
import math
import jax
import jax.numpy as jnp
from jax import lax

C = 384
HID = 1536
KS = 7
BAND_MAX = 32
H = 256
W = 512
ROWS_BUF = 512
N_LAT = 16


def draw_band_rows(key, part):
    first_key, second_key = jax.random.split(jax.random.fold_in(key, 17))
    count = N_LAT
    maximum_surplus = BAND_MAX - 3
    remaining = H - 3 * count - maximum_surplus
    largest_band_rows = jax.random.randint(first_key, (), 0, count)
    band_position = jnp.arange(count, dtype=jnp.int32)
    shares = jax.random.randint(second_key, (count,), 2, 4)
    shares = jnp.where(band_position == largest_band_rows, 0, shares)
    base_rows_each = remaining * shares // jnp.sum(shares)
    remainder_rows = remaining - jnp.sum(base_rows_each)
    peer_rank = jnp.where(band_position > largest_band_rows, band_position - 1, band_position)
    added_row_count = jnp.where((band_position != largest_band_rows) & (peer_rank < remainder_rows), 1, 0)
    surplus_rows = jnp.where(band_position == largest_band_rows, maximum_surplus, base_rows_each + added_row_count)
    return (3 + surplus_rows).astype(jnp.int32)


def with_ends(array, stream_key, least, top_value):
    spot = [jax.random.randint(jax.random.fold_in(stream_key, axis), (), 0, length) for axis, length in enumerate(array.shape)]
    main_axis = array.shape.index(max(array.shape))
    next_to = spot[:main_axis] + [(spot[main_axis] + 1) % array.shape[main_axis]] + spot[main_axis + 1:]
    return array.at[tuple(spot)].set(least).at[tuple(next_to)].set(top_value)


def block_levels(own_key, shape, cuts, least, top_value):
    loudness, own = 1.0, jax.random.fold_in(own_key, 6)
    for dim, shards_of in cuts:
        heights = jnp.exp(jax.random.uniform(jax.random.fold_in(own, dim), (shards_of,), jnp.float32, least / len(cuts), top_value / len(cuts)))
        loudness = loudness * jnp.repeat(heights, shape[dim] // shards_of).reshape([-1 if axis == dim else 1 for axis in range(len(shape))])
    return loudness


def normal_values(own_key, extent, scale, bound, pieces=(), held_as=jnp.bfloat16):
    values = scale * jax.random.normal(own_key, extent, jnp.float32)
    if pieces:
        values = values * block_levels(own_key, extent, pieces, -0.22, 0.18)
    return jnp.clip(values, -bound, bound).astype(held_as)


def setup_inputs(seed: int = 0) -> dict:
    key_list = jax.random.split(jax.random.key(seed), 13)
    return {
        "feature": normal_values(key_list[0], (ROWS_BUF, W, C), 1.0, 6.0, ((0, 16), (1, 16))),
        "coverage": with_ends((jax.random.randint(key_list[1], (ROWS_BUF, W), 0, 5) < 4).astype(jnp.int32), jax.random.fold_in(key_list[1], 1), 0, 1),
        "band_rows": draw_band_rows(jax.random.fold_in(key_list[12], 71), 0),
        "depth_weight": normal_values(key_list[3], (KS, KS, C), (KS * KS) ** -0.5, 0.875),
        "norm_gain": jnp.clip(1.0 + 0.15 * jax.random.normal(key_list[4], (C,), jnp.float32), 0.25, 1.75),
        "norm_shift": normal_values(key_list[5], (C,), 0.5, 3.0, (), jnp.float32),
        "up_weight": normal_values(key_list[6], (C, HID), C ** -0.5, 0.3125, ((0, 16),)),
        "up_bias": normal_values(key_list[7], (HID,), 0.5, 3.0, (), jnp.float32),
        "down_weight": normal_values(key_list[8], (HID, C), HID ** -0.5, 0.15625, ((0, 16),)),
        "down_bias": normal_values(key_list[9], (C,), 0.5, 3.0, (), jnp.float32),
        "layer_scale": jnp.clip(jnp.exp(jax.random.uniform(key_list[10], (C,), jnp.float32, math.log(0.3), math.log(1.5))), 0.3, 1.5),
        "cotangent": normal_values(key_list[11], (ROWS_BUF, W, C), 1.0, 6.0, ((0, 16), (1, 16))),
    }


SQRT_TWO_PI = 0.7978845608028654
CUBIC = 0.044715
EPSILON = 1e-06

def smooth_gate(pre_act):
    argument = SQRT_TWO_PI * (pre_act + CUBIC * pre_act * pre_act * pre_act)
    return 0.5 * pre_act * (1.0 + jnp.tanh(argument))

def smooth_slope(pre_act):
    argument = SQRT_TWO_PI * (pre_act + CUBIC * pre_act * pre_act * pre_act)
    tangent = jnp.tanh(argument)
    return 0.5 * (1.0 + tangent) + 0.5 * pre_act * (1.0 - tangent * tangent) * SQRT_TWO_PI * (1.0 + 3.0 * CUBIC * pre_act * pre_act)

def token_block(depth_out, inputs, cot_rows, norm_gain, norm_shift, up_weight, up_bias, down_weight, down_bias, layer_scale):
    center = lax.optimization_barrier(jnp.mean(depth_out, axis=-1, keepdims=True))
    offset = depth_out - center
    scale_inv = lax.rsqrt(lax.optimization_barrier(jnp.mean(offset * offset, axis=-1, keepdims=True)) + EPSILON)
    standard = offset * scale_inv
    normed = (standard * norm_gain + norm_shift).astype(jnp.bfloat16)
    before = jnp.dot(normed, up_weight, preferred_element_type=jnp.float32) + up_bias
    active = smooth_gate(before).astype(jnp.bfloat16)
    branch = jnp.dot(active, down_weight, preferred_element_type=jnp.float32) + down_bias
    result = (inputs.astype(jnp.float32) + layer_scale * branch).astype(jnp.bfloat16)
    upstream = (layer_scale * cot_rows.astype(jnp.float32)).astype(jnp.bfloat16)
    sum_down = lax.dot_general(active, upstream, (((0,), (0,)), ((), ())), preferred_element_type=jnp.float32)
    back_active = lax.dot_general(upstream, down_weight, (((1,), (1,)), ((), ())), preferred_element_type=jnp.float32)
    back_before = (back_active * smooth_slope(before)).astype(jnp.bfloat16)
    sum_up = lax.dot_general(normed, back_before, (((0,), (0,)), ((), ())), preferred_element_type=jnp.float32)
    back_normed = lax.dot_general(back_before, up_weight, (((1,), (1,)), ((), ())), preferred_element_type=jnp.float32)
    back_unit = back_normed * norm_gain
    back_depth = scale_inv * (back_unit - lax.optimization_barrier(jnp.mean(back_unit, axis=-1, keepdims=True)) - standard * lax.optimization_barrier(jnp.mean(back_unit * standard, axis=-1, keepdims=True)))
    return (result, back_depth.astype(jnp.bfloat16), sum_up, sum_down)

def border(field):
    rows_padded = jnp.pad(field, ((3, 3), (0, 0), (0, 0)))
    return jnp.concatenate([rows_padded[:, -3:], rows_padded, rows_padded[:, :3]], axis=1)

def reference(feature, coverage, band_rows, depth_weight, norm_gain, norm_shift, up_weight, up_bias, down_weight, down_bias, layer_scale, cotangent):
    starts = (jnp.cumsum(band_rows) - band_rows).astype(jnp.int32)
    row_index = jnp.arange(H, dtype=jnp.int32)
    band_of_row = (lax.optimization_barrier(jnp.sum((row_index[:, None] >= starts[None, :]).astype(jnp.int32), axis=1)) - 1).astype(jnp.int32)
    slot_of_row = (band_of_row * BAND_MAX + row_index - jnp.take(starts, band_of_row)).astype(jnp.int32)
    map_rows = jnp.take(feature, slot_of_row, axis=0)
    covered = jnp.take(coverage, slot_of_row, axis=0).astype(jnp.bfloat16)
    cot_map = jnp.take(cotangent, slot_of_row, axis=0)
    masked = map_rows * covered[:, :, None]
    padded = border(masked)
    depth_out = jnp.zeros((H, W, C), jnp.float32)
    for row_off in range(KS):
        for col_off in range(KS):
            depth_out = depth_out + padded[row_off:row_off + H, col_off:col_off + W].astype(jnp.float32) * depth_weight[row_off, col_off].astype(jnp.float32)
    block_rows = 8
    blocks = H // block_rows

    def scan_step(totals, block_id):
        first_row = (block_id * block_rows).astype(jnp.int32)
        depth_rows = lax.dynamic_slice_in_dim(depth_out, first_row, block_rows, 0).reshape(-1, C)
        input_rows = lax.dynamic_slice_in_dim(map_rows, first_row, block_rows, 0).reshape(-1, C)
        cot_rows = lax.dynamic_slice_in_dim(cot_map, first_row, block_rows, 0).reshape(-1, C)
        result, back_depth, sum_up, sum_down = token_block(depth_rows, input_rows, cot_rows, norm_gain, norm_shift, up_weight, up_bias, down_weight, down_bias, layer_scale)
        return ((totals[0] + sum_up, totals[1] + sum_down), (result.reshape(block_rows, W, C), back_depth.reshape(block_rows, W, C)))
    start_totals = (jnp.zeros((C, HID), jnp.float32), jnp.zeros((HID, C), jnp.float32))
    (sum_up, sum_down), (result, back_depth) = lax.scan(scan_step, start_totals, jnp.arange(blocks, dtype=jnp.int32))
    result = result.reshape(H, W, C)
    back_depth = back_depth.reshape(H, W, C)
    padded_back = border(back_depth)
    spread = jnp.zeros((H, W, C), jnp.float32)
    tap_list = []
    for row_off in range(KS):
        for col_off in range(KS):
            spread = spread + padded_back[6 - row_off:6 - row_off + H, 6 - col_off:6 - col_off + W].astype(jnp.float32) * depth_weight[row_off, col_off].astype(jnp.float32)
            tap_list.append(lax.optimization_barrier(jnp.sum(padded[row_off:row_off + H, col_off:col_off + W].astype(jnp.float32) * back_depth.astype(jnp.float32), axis=(0, 1))))
    grad_map = (cot_map.astype(jnp.float32) + covered.astype(jnp.float32)[:, :, None] * spread).astype(jnp.bfloat16)
    rscale = 1.0 / math.sqrt(H * W)
    slot_index = jnp.arange(ROWS_BUF, dtype=jnp.int32)
    owner_band = (slot_index // BAND_MAX).astype(jnp.int32)
    slot_in_band = (slot_index % BAND_MAX).astype(jnp.int32)
    used = slot_in_band < jnp.take(band_rows, owner_band)
    source = jnp.clip(jnp.take(starts, owner_band) + slot_in_band, 0, H - 1).astype(jnp.int32)
    block_out = jnp.where(used[:, None, None], jnp.take(result, source, axis=0), jnp.zeros((), jnp.bfloat16)).astype(jnp.bfloat16)
    grad_in = jnp.where(used[:, None, None], jnp.take(grad_map, source, axis=0), jnp.zeros((), jnp.bfloat16)).astype(jnp.bfloat16)
    grad_depth = jnp.stack(tap_list, axis=0).reshape(KS, KS, C) * rscale
    return (block_out, grad_in, sum_up * rscale, sum_down * rscale, grad_depth)
```

```python
import functools
import math

import jax
import jax.numpy as jnp
from jax import lax
from jax.experimental import pallas as pl
from jax.experimental.pallas import tpu as pltpu
from jax.sharding import PartitionSpec as P

BAND_MEAN = 16


SQRT_TWO_PI = 0.7978845608028654
CUBIC = 0.044715
EPSILON = 1e-06


def padded(array, sides, width):
    for axis, dim in sides:
        size, length = (lax.axis_size(axis), array.shape[dim])
        up = [(i, (i + 1) % size) for i in range(size)]
        down = [(j, i) for i, j in up]
        last = lax.slice_in_dim(array, length - width, length, axis=dim)
        initial = lax.slice_in_dim(array, 0, width, axis=dim)
        before = lax.ppermute(last, axis, up)
        after = lax.ppermute(initial, axis, down)
        array = jnp.concatenate([before, array, after], axis=dim)
    return array


def shifted(block, axis, distance):
    devices = range(lax.axis_size(axis))
    route = [(i - distance, i) for i in devices if i - distance in devices]
    return lax.ppermute(block, axis, route)


def smooth_gate(pre_act):
    argument = SQRT_TWO_PI * (pre_act + CUBIC * pre_act * pre_act * pre_act)
    return 0.5 * pre_act * (1.0 + jnp.tanh(argument))


def smooth_slope(pre_act):
    argument = SQRT_TWO_PI * (pre_act + CUBIC * pre_act * pre_act * pre_act)
    tangent = jnp.tanh(argument)
    return 0.5 * (1.0 + tangent) + 0.5 * pre_act * (1.0 - tangent * tangent) * SQRT_TWO_PI * (
        1.0 + 3.0 * CUBIC * pre_act * pre_act
    )


def extend(field, live_rows):
    widened = padded(field, (("lon", 1),), 3)
    last_rows = lax.dynamic_slice_in_dim(widened, live_rows - 3, 3, 0)
    from_above = shifted(last_rows, "lat", 1)
    from_below = shifted(widened[:3], "lat", -1)
    zero_rows = jnp.zeros((3,) + widened.shape[1:], widened.dtype)
    stacked = jnp.concatenate([from_above, widened, zero_rows], axis=0)
    return lax.dynamic_update_slice_in_dim(stacked, from_below, live_rows + 3, 0)


def places():
    lat, lon = lax.axis_index("lat"), lax.axis_index("lon")
    return lat, lon, lat // 4, (lat // 2) % 2, lat % 2, lon // 8, lon % 8


def remote(src, dst, sends, recvs, slot, device):
    return pltpu.make_async_remote_copy(
        src_ref=src,
        dst_ref=dst,
        send_sem=sends.at[slot],
        recv_sem=recvs.at[slot],
        device_id=device,
        device_id_type=pl.DeviceIdType.MESH,
    )


def greet(peers):
    barrier = pltpu.get_barrier_semaphore()
    for peer in peers:
        pl.semaphore_signal(barrier, inc=1, device_id=peer, device_id_type=pl.DeviceIdType.MESH)
    pl.semaphore_wait(barrier, len(peers))


def gather_kernel(up_ref, down_ref, full_up, full_down, sends, recvs):
    lat, lon, x, yh, c, yl, z = places()
    loop = [(lat, yl * 8 + (z + k) % 8) for k in range(1, 8)]
    across = (lat, (1 - yl) * 8 + z)
    twin = (lat + 1 - 2 * c, lon)
    greet(loop + [across, twin])

    def parts(up, down, block, half):
        lanes = pl.ds(pl.multiple_of(half * 768, 768), 768)
        return (
            up.at[pl.ds(block * 3, 3), :, lanes],
            down.at[pl.ds(block * 12 + half * 6, 6)],
        )

    def copies(block, half, base, device, own=False):
        sources = parts(up_ref, down_ref, 0, half) if own else parts(full_up, full_down, block, half)
        targets = parts(full_up, full_down, block, half)
        return [
            remote(sources[i], targets[i], sends, recvs, base * 2 + i, device) for i in range(2)
        ]

    started = []

    def launch(pair):
        for copy in pair:
            copy.start()
        started.extend(pair)

    for k in (4, 3, 5, 2, 6, 1, 7):
        launch(copies(lon, c, k - 1, loop[k - 1], own=True))
    launch(copies(lon, c, 7, across, own=True))
    full_up[pl.ds(lon * 3, 3)] = up_ref[...]
    full_down[pl.ds(lon * 12, 12)] = down_ref[...]
    for k in (1, 7, 2, 6, 3, 5, 4):
        block = yl * 8 + (z + 8 - k) % 8
        for copy in copies(block, c, k - 1, across):
            copy.wait_recv()
        launch(copies(block, c, 7 + k, across))
        launch(copies(block, c, 14 + k, twin))
    for k in (0, 1, 7, 2, 6, 3, 5, 4):
        block = (1 - yl) * 8 + (z + 8 - k) % 8
        for copy in copies(block, c, 7 + k, across):
            copy.wait_recv()
        launch(copies(block, c, 22 + k, twin))
    for k in range(1, 8):
        block = yl * 8 + (z + 8 - k) % 8
        for copy in copies(block, 1 - c, 14 + k, twin):
            copy.wait_recv()
    for k in range(8):
        block = (1 - yl) * 8 + (z + 8 - k) % 8
        for copy in copies(block, 1 - c, 22 + k, twin):
            copy.wait_recv()
    for copy in started:
        copy.wait_send()


def gather_weights(up_weight, down_weight):
    vmem = pl.BlockSpec(memory_space=pltpu.VMEM)
    full_up, full_down = pl.pallas_call(
        gather_kernel,
        out_shape=(
            jax.ShapeDtypeStruct((48, 8, 1536), jnp.bfloat16),
            jax.ShapeDtypeStruct((192, 8, 384), jnp.bfloat16),
        ),
        in_specs=[vmem, vmem],
        out_specs=(vmem, vmem),
        scratch_shapes=[pltpu.SemaphoreType.DMA((60,)), pltpu.SemaphoreType.DMA((60,))],
        compiler_params=pltpu.CompilerParams(collective_id=1, has_side_effects=True),
        name="gather_weights",
    )(up_weight.reshape(3, 8, 1536), down_weight.reshape(12, 8, 384))
    return full_up.reshape(384, 1536), full_down.reshape(1536, 384)


def sum_kernel(
    rscale, up_ref, down_ref, up_out, down_out, twin_send, twin_recv, x_send, x_recv,
    total, y_send, y_recv, z_send, z_recv, h_send, h_recv, pieces, others, sends, recvs,
):
    lat, lon, x, yh, c, yl, z = places()
    f32, bf16 = jnp.float32, jnp.bfloat16
    twin = (lat + 1 - 2 * c, lon)
    column = [(((x + k) % 4) * 4 + yh * 2 + c, lon) for k in range(1, 4)]
    across = (lat, (1 - yl) * 8 + z)
    loop = [(lat, yl * 8 + (z + k) % 8) for k in range(1, 8)]
    far = (lat + 2 - 4 * yh, lon)
    greet([twin] + column + [across] + loop + [far])
    started = []

    def launch(copy):
        copy.start()
        started.append(copy)
        return copy

    order = (2, 1, 3, 0)

    def chunk_of(k):
        return (x + k) % 4

    def up_part(part):
        return up_ref[:, :, pl.ds(pl.multiple_of(part * 384, 384), 384)]

    twin_copies = {}
    for k in order:
        part = chunk_of(k)

        @pl.when(c == 1)
        def _():
            twin_send[k] = up_part(part).astype(bf16)

        @pl.when(c == 0)
        def _():
            @pl.loop(0, 16)
            def _(block):
                twin_send[k, pl.ds(block * 3, 3)] = down_ref[
                    pl.ds(block * 12 + part * 3, 3)
                ].astype(bf16)

        twin_copies[k] = launch(
            remote(twin_send.at[k], twin_recv.at[k], sends, recvs, k, twin)
        )
    for k in order:
        part = chunk_of(k)
        twin_copies[k].wait_recv()

        @pl.when(c == 0)
        def _():
            total[...] = up_part(part) + twin_recv[k].astype(f32)

        @pl.when(c == 1)
        def _():
            @pl.loop(0, 16)
            def _(block):
                total[pl.ds(block * 3, 3)] = down_ref[
                    pl.ds(block * 12 + part * 3, 3)
                ] + twin_recv[k, pl.ds(block * 3, 3)].astype(f32)

        if k:
            x_send[k - 1] = total[...].astype(bf16)
            launch(
                remote(x_send.at[k - 1], x_recv.at[k - 1], sends, recvs, 3 + k, column[k - 1])
            )
    for k in (1, 3, 2):
        remote(x_send.at[k - 1], x_recv.at[k - 1], sends, recvs, 3 + k, column[k - 1]).wait_recv()
    far_half = pl.ds((1 - yl) * 24, 24)
    near_half = pl.ds(yl * 24, 24)

    def summed(rows):
        return total[rows] + (
            x_recv[0, rows].astype(f32) + x_recv[1, rows].astype(f32) + x_recv[2, rows].astype(f32)
        )

    y_send[...] = summed(far_half).astype(bf16)
    y_copy = launch(remote(y_send, y_recv, sends, recvs, 7, across))
    total[near_half] = summed(near_half)
    y_copy.wait_recv()
    for k in (4, 3, 5, 2, 6, 1, 7):
        zk = (z + k) % 8
        z_send[k - 1] = (
            total[pl.ds(yl * 24 + zk * 3, 3)] + y_recv[pl.ds(zk * 3, 3)].astype(f32)
        ).astype(bf16)
        launch(remote(z_send.at[k - 1], z_recv.at[k - 1], sends, recvs, 7 + k, loop[k - 1]))
    piece = total[pl.ds(yl * 24 + z * 3, 3)] + y_recv[pl.ds(z * 3, 3)].astype(f32)
    for k in (1, 7, 2, 6, 3, 5, 4):
        remote(z_send.at[k - 1], z_recv.at[k - 1], sends, recvs, 7 + k, loop[k - 1]).wait_recv()
        piece = piece + z_recv[k - 1].astype(f32)
    h_send[...] = piece
    far_copy = launch(remote(h_send, h_recv, sends, recvs, 15, far))
    far_copy.wait_recv()
    pieces[x] = (piece + h_recv[...]) * rscale
    for k in range(1, 4):
        launch(remote(pieces.at[x], pieces.at[x], sends, recvs, 15 + k, column[k - 1]))
    for k in range(1, 4):
        owner = (x + 4 - k) % 4
        remote(
            pieces.at[owner], pieces.at[owner], sends, recvs, 15 + k, column[k - 1]
        ).wait_recv()
    last = launch(remote(pieces, others, sends, recvs, 19, twin))
    last.wait_recv()

    def place(ups, downs):
        for part in range(4):
            up_out[:, :, part * 384 : part * 384 + 384] = ups[part]
            down_out[part * 3 : part * 3 + 3] = downs[part]

    @pl.when(c == 0)
    def _():
        place(pieces, others)

    @pl.when(c == 1)
    def _():
        place(others, pieces)

    for copy in started:
        copy.wait_send()


def sum_weights(sum_up, sum_down, rscale):
    vmem = pl.BlockSpec(memory_space=pltpu.VMEM)
    f32, bf16 = jnp.float32, jnp.bfloat16
    up_part, down_part = pl.pallas_call(
        functools.partial(sum_kernel, rscale),
        out_shape=(
            jax.ShapeDtypeStruct((3, 8, 1536), f32),
            jax.ShapeDtypeStruct((12, 8, 384), f32),
        ),
        in_specs=[vmem, vmem],
        out_specs=(vmem, vmem),
        scratch_shapes=[
            pltpu.VMEM((4, 48, 8, 384), bf16),
            pltpu.VMEM((4, 48, 8, 384), bf16),
            pltpu.VMEM((3, 48, 8, 384), bf16),
            pltpu.VMEM((3, 48, 8, 384), bf16),
            pltpu.VMEM((48, 8, 384), f32),
            pltpu.VMEM((24, 8, 384), bf16),
            pltpu.VMEM((24, 8, 384), bf16),
            pltpu.VMEM((7, 3, 8, 384), bf16),
            pltpu.VMEM((7, 3, 8, 384), bf16),
            pltpu.VMEM((3, 8, 384), f32),
            pltpu.VMEM((3, 8, 384), f32),
            pltpu.VMEM((4, 3, 8, 384), f32),
            pltpu.VMEM((4, 3, 8, 384), f32),
            pltpu.SemaphoreType.DMA((20,)),
            pltpu.SemaphoreType.DMA((20,)),
        ],
        compiler_params=pltpu.CompilerParams(collective_id=2, has_side_effects=True),
        name="sum_weights",
    )(sum_up.reshape(48, 8, 1536), sum_down.reshape(192, 8, 384))
    return up_part.reshape(24, 1536), down_part.reshape(96, 384)


def taps_kernel(
    rscale, taps_ref, out_ref, first, twin_recv, columns, h_send, h_recv, y_send, y_recv,
    z_send, z_recv, gathered, sends, recvs,
):
    lat, lon, x, yh, c, yl, z = places()
    twin = (lat + 1 - 2 * c, lon)
    column = [(((x + k) % 4) * 4 + yh * 2 + c, lon) for k in range(1, 4)]
    across = (lat, (1 - yl) * 8 + z)
    loop = [(lat, yl * 8 + (z + k) % 8) for k in range(1, 8)]
    far = (lat + 2 - 4 * yh, lon)
    greet([twin] + column + [across] + loop + [far])
    started = []

    def launch(copy):
        copy.start()
        started.append(copy)
        return copy

    launch(remote(taps_ref, twin_recv, sends, recvs, 0, twin)).wait_recv()
    columns[x] = taps_ref[...] + twin_recv[...]
    for k in range(1, 4):
        launch(remote(columns.at[x], columns.at[x], sends, recvs, k, column[k - 1]))
    for k in (1, 3, 2):
        owner = (x + 4 - k) % 4
        remote(columns.at[owner], columns.at[owner], sends, recvs, k, column[k - 1]).wait_recv()
    h_send[...] = (columns[0] + columns[1]) + (columns[2] + columns[3])
    launch(remote(h_send, h_recv, sends, recvs, 4, far)).wait_recv()
    y_send[...] = h_send[...] + h_recv[...]
    launch(remote(y_send, y_recv, sends, recvs, 5, across)).wait_recv()
    z_send[...] = y_send[...] + y_recv[...]
    for k in (4, 3, 5, 2, 6, 1, 7):
        launch(
            remote(z_send.at[(z + k) % 8], z_recv.at[k - 1], sends, recvs, 5 + k, loop[k - 1])
        )
    block = z_send[z]
    for k in (1, 7, 2, 6, 3, 5, 4):
        remote(z_send.at[z], z_recv.at[k - 1], sends, recvs, 5 + k, loop[k - 1]).wait_recv()
        block = block + z_recv[k - 1]
    gathered[z] = block * rscale
    for k in (4, 3, 5, 2, 6, 1, 7):
        launch(remote(gathered.at[z], gathered.at[z], sends, recvs, 12 + k, loop[k - 1]))
    for k in (1, 7, 2, 6, 3, 5, 4):
        owner = (z + 8 - k) % 8
        remote(gathered.at[owner], gathered.at[owner], sends, recvs, 12 + k, loop[k - 1]).wait_recv()
    out_ref[...] = gathered[...]
    for copy in started:
        copy.wait_send()


def sum_taps(taps, rscale):
    vmem = pl.BlockSpec(memory_space=pltpu.VMEM)
    f32 = jnp.float32
    whole = pltpu.VMEM((8, 8, 384), f32)
    return pl.pallas_call(
        functools.partial(taps_kernel, rscale),
        out_shape=jax.ShapeDtypeStruct((8, 8, 384), f32),
        in_specs=[vmem],
        out_specs=vmem,
        scratch_shapes=[
            whole,
            whole,
            pltpu.VMEM((4, 8, 8, 384), f32),
            whole,
            whole,
            whole,
            whole,
            whole,
            pltpu.VMEM((7, 8, 384), f32),
            whole,
            pltpu.SemaphoreType.DMA((20,)),
            pltpu.SemaphoreType.DMA((20,)),
        ],
        compiler_params=pltpu.CompilerParams(collective_id=3, has_side_effects=True),
        name="sum_taps",
    )(taps)


def shards(
    feature,
    coverage,
    band_rows,
    depth_weight,
    norm_gain,
    norm_shift,
    up_weight,
    up_bias,
    down_weight,
    down_bias,
    layer_scale,
    cotangent,
):
    rows_max, tile_cols, channels = feature.shape
    kernel = depth_weight.shape[0]
    live_rows = lax.dynamic_index_in_dim(band_rows, lax.axis_index("lat"), 0, keepdims=False)
    inside = jnp.arange(rows_max, dtype=jnp.int32) < live_rows
    covered = jnp.where(inside[:, None], coverage, 0).astype(jnp.bfloat16)
    masked = feature * covered[:, :, None]
    framed = extend(masked, live_rows)
    depth_out = jnp.zeros((rows_max, tile_cols, channels), jnp.float32)
    for row_off in range(kernel):
        for col_off in range(kernel):
            depth_out = depth_out + framed[
                row_off : row_off + rows_max, col_off : col_off + tile_cols
            ].astype(jnp.float32) * depth_weight[row_off, col_off].astype(jnp.float32)
    full_up, full_down = gather_weights(up_weight, down_weight)
    depth_rows = depth_out.reshape(-1, channels)
    center = jnp.mean(depth_rows, axis=-1, keepdims=True)
    offset = depth_rows - center
    scale_inv = lax.rsqrt(jnp.mean(offset * offset, axis=-1, keepdims=True) + EPSILON)
    standard = offset * scale_inv
    normed = (standard * norm_gain + norm_shift).astype(jnp.bfloat16)
    before = jnp.dot(normed, full_up, preferred_element_type=jnp.float32) + up_bias
    active = smooth_gate(before).astype(jnp.bfloat16)
    branch = jnp.dot(active, full_down, preferred_element_type=jnp.float32) + down_bias
    result = (feature.reshape(-1, channels).astype(jnp.float32) + layer_scale * branch).astype(
        jnp.bfloat16
    )
    cot_live = jnp.where(inside[:, None, None], cotangent, jnp.zeros_like(cotangent)).reshape(
        -1, channels
    )
    upstream = (layer_scale * cot_live.astype(jnp.float32)).astype(jnp.bfloat16)
    sum_down = lax.dot_general(
        active, upstream, (((0,), (0,)), ((), ())), preferred_element_type=jnp.float32
    )
    back_active = lax.dot_general(
        upstream, full_down, (((1,), (1,)), ((), ())), preferred_element_type=jnp.float32
    )
    back_before = (back_active * smooth_slope(before)).astype(jnp.bfloat16)
    sum_up = lax.dot_general(
        normed, back_before, (((0,), (0,)), ((), ())), preferred_element_type=jnp.float32
    )
    back_normed = lax.dot_general(
        back_before, full_up, (((1,), (1,)), ((), ())), preferred_element_type=jnp.float32
    )
    back_unit = back_normed * norm_gain
    back_depth = scale_inv * (
        back_unit
        - jnp.mean(back_unit, axis=-1, keepdims=True)
        - standard * jnp.mean(back_unit * standard, axis=-1, keepdims=True)
    )
    back_depth = back_depth.astype(jnp.bfloat16).reshape(rows_max, tile_cols, channels)
    framed_back = extend(back_depth, live_rows)
    spread = jnp.zeros((rows_max, tile_cols, channels), jnp.float32)
    tap_list = []
    for row_off in range(kernel):
        for col_off in range(kernel):
            spread = spread + framed_back[
                6 - row_off : 6 - row_off + rows_max, 6 - col_off : 6 - col_off + tile_cols
            ].astype(jnp.float32) * depth_weight[row_off, col_off].astype(jnp.float32)
            tap_list.append(
                jnp.sum(
                    framed[row_off : row_off + rows_max, col_off : col_off + tile_cols].astype(
                        jnp.float32
                    )
                    * back_depth.astype(jnp.float32),
                    axis=(0, 1),
                )
            )
    grad_local = (
        cotangent.astype(jnp.float32) + covered.astype(jnp.float32)[:, :, None] * spread
    ).astype(jnp.bfloat16)
    grad_in = jnp.where(inside[:, None, None], grad_local, jnp.zeros_like(grad_local))
    block_out = jnp.where(
        inside[:, None, None],
        result.reshape(rows_max, tile_cols, channels),
        jnp.zeros_like(feature),
    )
    rscale = 1.0 / math.sqrt(BAND_MEAN * lax.axis_size("lat") * tile_cols * lax.axis_size("lon"))
    tap_list.extend([jnp.zeros_like(tap_list[0])] * (64 - kernel * kernel))
    tap_terms = jnp.stack(tap_list, axis=0).reshape(8, 8, channels)
    grad_depth = sum_taps(tap_terms, rscale).reshape(64, channels)[: kernel * kernel]
    up_part, down_part = sum_weights(sum_up, sum_down, rscale)
    return (block_out, grad_in, up_part, down_part, grad_depth.reshape(kernel, kernel, channels))


def solution(mesh):
    placed = (
        P("lat", "lon", None),
        P("lat", "lon"),
        P(),
        P(),
        P(),
        P(),
        P("lon", None),
        P(),
        P("lon", None),
        P(),
        P(),
        P("lat", "lon", None),
    )
    return jax.shard_map(
        shards,
        mesh=mesh,
        in_specs=placed,
        out_specs=(
            P("lat", "lon", None),
            P("lat", "lon", None),
            P("lon", None),
            P("lon", None),
            P(),
        ),
        check_vma=False,
    )
```

```python
import functools
import math

import jax
import jax.numpy as jnp
from jax import lax
from jax.experimental import pallas as pl
from jax.experimental.pallas import tpu as pltpu
from jax.sharding import PartitionSpec as P

BAND_MEAN = 16


SQRT_TWO_PI = 0.7978845608028654
CUBIC = 0.044715
EPSILON = 1e-06


def smooth_gate(pre_act):
    argument = SQRT_TWO_PI * (pre_act + CUBIC * pre_act * pre_act * pre_act)
    return 0.5 * pre_act * (1.0 + jnp.tanh(argument))


def smooth_slope(pre_act):
    argument = SQRT_TWO_PI * (pre_act + CUBIC * pre_act * pre_act * pre_act)
    tangent = jnp.tanh(argument)
    return 0.5 * (1.0 + tangent) + 0.5 * pre_act * (1.0 - tangent * tangent) * SQRT_TWO_PI * (
        1.0 + 3.0 * CUBIC * pre_act * pre_act
    )


def places():
    lat, lon = lax.axis_index("lat"), lax.axis_index("lon")
    return lat, lon, lat // 4, (lat // 2) % 2, lat % 2, lon // 8, lon % 8


def remote(src, dst, sends, recvs, slot, device):
    return pltpu.make_async_remote_copy(
        src_ref=src,
        dst_ref=dst,
        send_sem=sends.at[slot],
        recv_sem=recvs.at[slot],
        device_id=device,
        device_id_type=pl.DeviceIdType.MESH,
    )


def greet(peers):
    barrier = pltpu.get_barrier_semaphore()
    for peer in peers:
        pl.semaphore_signal(barrier, inc=1, device_id=peer, device_id_type=pl.DeviceIdType.MESH)
    pl.semaphore_wait(barrier, len(peers))


def halo_peers(lat, lon):
    north, south = (lat + 15) % 16, (lat + 1) % 16
    west, east = (lon + 15) % 16, (lon + 1) % 16
    return [
        (lat, east), (lat, west), (south, lon), (north, lon),
        (south, east), (south, west), (north, east), (north, west),
    ]


def halo_copies(edges, arrivals, sends, recvs, base, peers):
    return [
        remote(edges[i], arrivals[i], sends, recvs, base + i, peers[i]) for i in range(8)
    ]


def halo_edges(field, live_rows):
    final = lax.dynamic_slice_in_dim(field, live_rows - 3, 3, 0)
    first = field[:3]
    return [
        field[:, -3:], field[:, :3], final, first,
        final[:, -3:], final[:, :3], first[:, -3:], first[:, :3],
    ]


def halo_shapes(rows, cols, channels):
    tall = jax.ShapeDtypeStruct((rows, 3, channels), jnp.bfloat16)
    wide = jax.ShapeDtypeStruct((3, cols, channels), jnp.bfloat16)
    corner = jax.ShapeDtypeStruct((3, 3, channels), jnp.bfloat16)
    return [tall, tall, wide, wide, corner, corner, corner, corner]


def framed_by(field, arrivals, live_rows):
    west, east, north, south, nw, ne, sw, se = arrivals
    lat = lax.axis_index("lat")
    above = jnp.concatenate([nw, north, ne], axis=1)
    below = jnp.concatenate([sw, south, se], axis=1)
    above = jnp.where(lat > 0, above, jnp.zeros_like(above))
    below = jnp.where(lat < lax.axis_size("lat") - 1, below, jnp.zeros_like(below))
    widened = jnp.concatenate([west, field, east], axis=1)
    stacked = jnp.concatenate([above, widened, jnp.zeros_like(above)], axis=0)
    return lax.dynamic_update_slice_in_dim(stacked, below, live_rows + 3, 0)


def gather_kernel(*refs):
    up_ref, down_ref = refs[:2]
    edges = refs[2:10]
    full_up, full_down = refs[10:12]
    arrivals = refs[12:20]
    sends, recvs = refs[20:]
    lat, lon, x, yh, c, yl, z = places()
    after = (lat, yl * 8 + (z + 1) % 8)
    ahead = (lat, yl * 8 + (z + 7) % 8)
    across = (lat, (1 - yl) * 8 + z)
    twin = (lat + 1 - 2 * c, lon)
    around = halo_peers(lat, lon)
    greet([after, ahead, across, twin] + around)
    started = []

    def parts(up, down, block, half):
        lanes = pl.ds(pl.multiple_of(half * 768, 768), 768)
        return (
            up.at[pl.ds(block * 3, 3), :, lanes],
            down.at[pl.ds(block * 12 + half * 6, 6)],
        )

    def copies(block, half, slot, device, own=False, which=(0, 1)):
        sources = parts(up_ref, down_ref, 0, half) if own else parts(full_up, full_down, block, half)
        targets = parts(full_up, full_down, block, half)
        return [
            remote(sources[i], targets[i], sends, recvs, slot * 2 + i, device) for i in which
        ]

    def mine(k):
        return yl * 8 + (z + 8 + k) % 8

    def theirs(k):
        return (1 - yl) * 8 + (z + 8 + k) % 8

    def send(block, slot, device, own=False, which=(0, 1)):
        for copy in copies(block, c, slot, device, own, which):
            copy.start()
            started.append(copy)

    def wait(block, slot, device, half=c, which=(0, 1)):
        for copy in copies(block, half, slot, device, False, which):
            copy.wait_recv()

    send(lon, 0, after, own=True)
    send(lon, 4, ahead, own=True)
    send(lon, 8, across, own=True)
    halos = halo_copies(edges, arrivals, sends, recvs, 64, around)
    for copy in halos:
        copy.start()
        started.append(copy)
    full_up[pl.ds(lon * 3, 3)] = up_ref[...]
    full_down[pl.ds(lon * 12, 12)] = down_ref[...]
    for k in (1, 2, 3):
        wait(mine(-k), k - 1, after)
        wait(mine(k), 3 + k, ahead)
        if k < 3:
            send(mine(-k), k, after)
            send(mine(k), 4 + k, ahead)
        else:
            send(mine(-3), 3, after, which=(0,))
            send(mine(3), 7, ahead, which=(1,))
        if k > 1:
            send(mine(-k), 7 + k, across)
            send(mine(k), 9 + k, across)
        send(mine(-k), 15 + k, twin)
        send(mine(k), 18 + k, twin)
        if k == 1:
            wait(theirs(0), 8, across)
            send(theirs(0), 14, after)
            send(theirs(0), 15, ahead)
            send(theirs(0), 23, twin)
    wait(theirs(-1), 14, after)
    wait(theirs(1), 15, ahead)
    send(theirs(-1), 24, twin)
    send(theirs(1), 25, twin)
    wait(mine(4), 3, after, which=(0,))
    wait(mine(4), 7, ahead, which=(1,))
    send(mine(4), 13, across)
    send(mine(4), 22, twin)
    for k in (2, 3):
        wait(theirs(-k), 7 + k, across)
        wait(theirs(k), 9 + k, across)
        send(theirs(-k), 24 + k, twin)
        send(theirs(k), 26 + k, twin)
    wait(theirs(4), 13, across)
    send(theirs(4), 30, twin)
    for k in (1, 2, 3):
        wait(mine(-k), 15 + k, twin, 1 - c)
        wait(mine(k), 18 + k, twin, 1 - c)
    wait(theirs(0), 23, twin, 1 - c)
    wait(theirs(-1), 24, twin, 1 - c)
    wait(theirs(1), 25, twin, 1 - c)
    wait(mine(4), 22, twin, 1 - c)
    for k in (2, 3):
        wait(theirs(-k), 24 + k, twin, 1 - c)
        wait(theirs(k), 26 + k, twin, 1 - c)
    wait(theirs(4), 30, twin, 1 - c)
    for copy in halos:
        copy.wait_recv()
    for copy in started:
        copy.wait_send()


def gather_weights(up_weight, down_weight, edges):
    vmem = pl.BlockSpec(memory_space=pltpu.VMEM)
    rows, cols, channels = edges[0].shape[0], edges[2].shape[1], edges[0].shape[2]
    full_up, full_down, *arrivals = pl.pallas_call(
        gather_kernel,
        out_shape=(
            jax.ShapeDtypeStruct((48, 8, 1536), jnp.bfloat16),
            jax.ShapeDtypeStruct((192, 8, 384), jnp.bfloat16),
            *halo_shapes(rows, cols, channels),
        ),
        in_specs=[vmem] * 10,
        out_specs=(vmem,) * 10,
        scratch_shapes=[pltpu.SemaphoreType.DMA((72,)), pltpu.SemaphoreType.DMA((72,))],
        compiler_params=pltpu.CompilerParams(collective_id=1, has_side_effects=True),
        name="gather_weights",
    )(up_weight.reshape(3, 8, 1536), down_weight.reshape(12, 8, 384), *edges)
    return full_up.reshape(384, 1536), full_down.reshape(1536, 384), arrivals


def sum_kernel(rscale, *refs):
    up_ref, down_ref, taps_ref = refs[:3]
    edges = refs[3:11]
    up_out, down_out, taps_out = refs[11:14]
    arrivals = refs[14:22]
    (
        twin_send, twin_recv, x_send, x_recv, d_send, d_recv, total, y_send, y_recv, z_send, z_recv,
        h_send, h_recv, pieces, others, tap_twin, tap_sum, tap_x, tap_ys, tap_yr, tap_z,
        tap_hs, tap_hr, sends, recvs,
    ) = refs[22:]
    lat, lon, x, yh, c, yl, z = places()
    f32, bf16 = jnp.float32, jnp.bfloat16
    twin = (lat + 1 - 2 * c, lon)
    column = [(((x + k) % 4) * 4 + yh * 2 + c, lon) for k in range(1, 4)]
    across = (lat, (1 - yl) * 8 + z)
    loop = [(lat, yl * 8 + (z + k) % 8) for k in range(1, 8)]
    far = (lat + 2 - 4 * yh, lon)
    around = halo_peers(lat, lon)
    greet([twin] + column + [across] + loop + [far] + around)
    started = []

    def launch(copy):
        copy.start()
        started.append(copy)
        return copy

    halos = [launch(copy) for copy in halo_copies(edges, arrivals, sends, recvs, 50, around)]
    tap_half = launch(
        remote(taps_ref.at[pl.ds((1 - c) * 4, 4)], tap_twin, sends, recvs, 22, twin)
    )
    order = (2, 1, 3, 0)

    def chunk_of(k):
        return (x + k) % 4

    def up_part(part):
        return up_ref[:, :, pl.ds(pl.multiple_of(part * 384, 384), 384)]

    twin_copies = {}
    for k in order:
        part = chunk_of(k)

        @pl.when(c == 1)
        def _():
            twin_send[k] = up_part(part).astype(bf16)

        @pl.when(c == 0)
        def _():
            @pl.loop(0, 16)
            def _(block):
                twin_send[k, pl.ds(block * 3, 3)] = down_ref[
                    pl.ds(block * 12 + part * 3, 3)
                ].astype(bf16)

        twin_copies[k] = launch(
            remote(twin_send.at[k], twin_recv.at[k], sends, recvs, k, twin)
        )
    upper, lower = pl.ds(0, 24), pl.ds(24, 24)
    for k in order:
        part = chunk_of(k)
        twin_copies[k].wait_recv()

        @pl.when(c == 0)
        def _():
            total[...] = up_part(part) + twin_recv[k].astype(f32)

        @pl.when(c == 1)
        def _():
            @pl.loop(0, 16)
            def _(block):
                total[pl.ds(block * 3, 3)] = down_ref[
                    pl.ds(block * 12 + part * 3, 3)
                ] + twin_recv[k, pl.ds(block * 3, 3)].astype(f32)

        if k == 2:
            d_send[...] = total[...].astype(bf16)
            via_next = launch(remote(d_send.at[upper], d_recv.at[0], sends, recvs, 20, column[0]))
            via_last = launch(remote(d_send.at[lower], d_recv.at[1], sends, recvs, 21, column[2]))
            tap_half.wait_recv()
            tap_sum[...] = taps_ref[pl.ds(c * 4, 4)] + tap_twin[...]
            for j in range(1, 4):
                launch(
                    remote(
                        tap_sum.at[(x + j) % 4], tap_x.at[j - 1], sends, recvs, 22 + j, column[j - 1]
                    )
                )
        elif k == 1:
            x_send[0, lower] = total[lower].astype(bf16)
            launch(remote(x_send.at[0, lower], x_recv.at[0, lower], sends, recvs, 4, column[0]))
            via_next.wait_recv()
            x_send[0, upper] = (total[upper] + d_recv[0].astype(f32)).astype(bf16)
            launch(remote(x_send.at[0, upper], x_recv.at[0, upper], sends, recvs, 5, column[0]))
        elif k == 3:
            x_send[1, upper] = total[upper].astype(bf16)
            launch(remote(x_send.at[1, upper], x_recv.at[1, upper], sends, recvs, 6, column[2]))
            via_last.wait_recv()
            x_send[1, lower] = (total[lower] + d_recv[1].astype(f32)).astype(bf16)
            launch(remote(x_send.at[1, lower], x_recv.at[1, lower], sends, recvs, 19, column[2]))
    for j in (1, 3, 2):
        remote(
            tap_sum.at[x], tap_x.at[j - 1], sends, recvs, 22 + j, column[j - 1]
        ).wait_recv()
    tap_ys[...] = (tap_sum[x] + tap_x[0]) + (tap_x[1] + tap_x[2])
    tap_y = launch(remote(tap_ys, tap_yr, sends, recvs, 26, across))
    tap_y.wait_recv()
    tap_z[z] = tap_ys[...] + tap_yr[...]
    for k in (4, 3, 5, 2, 6, 1, 7):
        launch(remote(tap_z.at[z], tap_z.at[z], sends, recvs, 26 + k, loop[k - 1]))
    remote(x_send.at[0, lower], x_recv.at[0, lower], sends, recvs, 4, column[0]).wait_recv()
    remote(x_send.at[0, upper], x_recv.at[0, upper], sends, recvs, 5, column[0]).wait_recv()
    remote(x_send.at[1, upper], x_recv.at[1, upper], sends, recvs, 6, column[2]).wait_recv()
    remote(x_send.at[1, lower], x_recv.at[1, lower], sends, recvs, 19, column[2]).wait_recv()
    far_half = pl.ds((1 - yl) * 24, 24)
    near_half = pl.ds(yl * 24, 24)

    def summed(rows):
        return total[rows] + (x_recv[0, rows].astype(f32) + x_recv[1, rows].astype(f32))

    y_send[...] = summed(far_half).astype(bf16)
    y_copy = launch(remote(y_send, y_recv, sends, recvs, 7, across))
    total[near_half] = summed(near_half)
    for k in (1, 7, 2, 6, 3, 5, 4):
        owner = (z + 8 - k) % 8
        remote(tap_z.at[owner], tap_z.at[owner], sends, recvs, 26 + k, loop[k - 1]).wait_recv()
    tap_hs[...] = ((tap_z[0] + tap_z[1]) + (tap_z[2] + tap_z[3])) + (
        (tap_z[4] + tap_z[5]) + (tap_z[6] + tap_z[7])
    )
    tap_h = launch(remote(tap_hs, tap_hr, sends, recvs, 34, far))
    y_copy.wait_recv()
    for k in (4, 3, 5, 2, 6, 1, 7):
        zk = (z + k) % 8
        z_send[k - 1] = (
            total[pl.ds(yl * 24 + zk * 3, 3)] + y_recv[pl.ds(zk * 3, 3)].astype(f32)
        ).astype(bf16)
        launch(remote(z_send.at[k - 1], z_recv.at[k - 1], sends, recvs, 7 + k, loop[k - 1]))
    piece = total[pl.ds(yl * 24 + z * 3, 3)] + y_recv[pl.ds(z * 3, 3)].astype(f32)
    tap_h.wait_recv()
    taps_out[c * 4 + x] = (tap_hs[...] + tap_hr[...]) * rscale
    for k in range(1, 4):
        launch(
            remote(
                taps_out.at[c * 4 + x], taps_out.at[c * 4 + x], sends, recvs, 34 + k, column[k - 1]
            )
        )
    for k in (1, 7, 2, 6, 3, 5, 4):
        remote(z_send.at[k - 1], z_recv.at[k - 1], sends, recvs, 7 + k, loop[k - 1]).wait_recv()
        piece = piece + z_recv[k - 1].astype(f32)
    h_send[...] = piece
    far_copy = launch(remote(h_send, h_recv, sends, recvs, 15, far))
    for k in range(1, 4):
        owner = c * 4 + (x + 4 - k) % 4
        remote(
            taps_out.at[owner], taps_out.at[owner], sends, recvs, 34 + k, column[k - 1]
        ).wait_recv()
    here, there = pl.ds(c * 4, 4), pl.ds((1 - c) * 4, 4)
    launch(remote(taps_out.at[here], taps_out.at[here], sends, recvs, 38, twin))
    far_copy.wait_recv()
    pieces[x] = (h_send[...] + h_recv[...]) * rscale
    for k in range(1, 4):
        launch(remote(pieces.at[x], pieces.at[x], sends, recvs, 15 + k, column[k - 1]))
    for k in range(1, 4):
        owner = (x + 4 - k) % 4
        remote(
            pieces.at[owner], pieces.at[owner], sends, recvs, 15 + k, column[k - 1]
        ).wait_recv()
    last = launch(remote(pieces, others, sends, recvs, 39, twin))
    remote(taps_out.at[there], taps_out.at[there], sends, recvs, 38, twin).wait_recv()
    for copy in halos:
        copy.wait_recv()
    last.wait_recv()

    def place(ups, downs):
        for part in range(4):
            up_out[:, :, part * 384 : part * 384 + 384] = ups[part]
            down_out[part * 3 : part * 3 + 3] = downs[part]

    @pl.when(c == 0)
    def _():
        place(pieces, others)

    @pl.when(c == 1)
    def _():
        place(others, pieces)

    for copy in started:
        copy.wait_send()


def sum_weights(sum_up, sum_down, taps, edges, rscale):
    vmem = pl.BlockSpec(memory_space=pltpu.VMEM)
    f32, bf16 = jnp.float32, jnp.bfloat16
    rows, cols, channels = edges[0].shape[0], edges[2].shape[1], edges[0].shape[2]
    up_part, down_part, taps, *arrivals = pl.pallas_call(
        functools.partial(sum_kernel, rscale),
        out_shape=(
            jax.ShapeDtypeStruct((3, 8, 1536), f32),
            jax.ShapeDtypeStruct((12, 8, 384), f32),
            jax.ShapeDtypeStruct((8, 8, 384), f32),
            *halo_shapes(rows, cols, channels),
        ),
        in_specs=[vmem] * 11,
        out_specs=(vmem,) * 11,
        scratch_shapes=[
            pltpu.VMEM((4, 48, 8, 384), bf16),
            pltpu.VMEM((4, 48, 8, 384), bf16),
            pltpu.VMEM((2, 48, 8, 384), bf16),
            pltpu.VMEM((2, 48, 8, 384), bf16),
            pltpu.VMEM((48, 8, 384), bf16),
            pltpu.VMEM((2, 24, 8, 384), bf16),
            pltpu.VMEM((48, 8, 384), f32),
            pltpu.VMEM((24, 8, 384), bf16),
            pltpu.VMEM((24, 8, 384), bf16),
            pltpu.VMEM((7, 3, 8, 384), bf16),
            pltpu.VMEM((7, 3, 8, 384), bf16),
            pltpu.VMEM((3, 8, 384), f32),
            pltpu.VMEM((3, 8, 384), f32),
            pltpu.VMEM((4, 3, 8, 384), f32),
            pltpu.VMEM((4, 3, 8, 384), f32),
            pltpu.VMEM((4, 8, 384), f32),
            pltpu.VMEM((4, 8, 384), f32),
            pltpu.VMEM((3, 8, 384), f32),
            pltpu.VMEM((8, 384), f32),
            pltpu.VMEM((8, 384), f32),
            pltpu.VMEM((8, 8, 384), f32),
            pltpu.VMEM((8, 384), f32),
            pltpu.VMEM((8, 384), f32),
            pltpu.SemaphoreType.DMA((58,)),
            pltpu.SemaphoreType.DMA((58,)),
        ],
        compiler_params=pltpu.CompilerParams(collective_id=2, has_side_effects=True),
        name="sum_weights",
    )(sum_up.reshape(48, 8, 1536), sum_down.reshape(192, 8, 384), taps, *edges)
    return up_part.reshape(24, 1536), down_part.reshape(96, 384), taps, arrivals


def shards(
    feature,
    coverage,
    band_rows,
    depth_weight,
    norm_gain,
    norm_shift,
    up_weight,
    up_bias,
    down_weight,
    down_bias,
    layer_scale,
    cotangent,
):
    rows_max, tile_cols, channels = feature.shape
    kernel = depth_weight.shape[0]
    live_rows = lax.dynamic_index_in_dim(band_rows, lax.axis_index("lat"), 0, keepdims=False)
    inside = jnp.arange(rows_max, dtype=jnp.int32) < live_rows
    covered = jnp.where(inside[:, None], coverage, 0).astype(jnp.bfloat16)
    masked = feature * covered[:, :, None]
    full_up, full_down, arrivals = gather_weights(
        up_weight, down_weight, halo_edges(masked, live_rows)
    )
    framed = framed_by(masked, arrivals, live_rows)
    depth_out = jnp.zeros((rows_max, tile_cols, channels), jnp.float32)
    for row_off in range(kernel):
        for col_off in range(kernel):
            depth_out = depth_out + framed[
                row_off : row_off + rows_max, col_off : col_off + tile_cols
            ].astype(jnp.float32) * depth_weight[row_off, col_off].astype(jnp.float32)
    depth_rows = depth_out.reshape(-1, channels)
    center = jnp.mean(depth_rows, axis=-1, keepdims=True)
    offset = depth_rows - center
    scale_inv = lax.rsqrt(jnp.mean(offset * offset, axis=-1, keepdims=True) + EPSILON)
    standard = offset * scale_inv
    normed = (standard * norm_gain + norm_shift).astype(jnp.bfloat16)
    before = jnp.dot(normed, full_up, preferred_element_type=jnp.float32) + up_bias
    active = smooth_gate(before).astype(jnp.bfloat16)
    branch = jnp.dot(active, full_down, preferred_element_type=jnp.float32) + down_bias
    result = (feature.reshape(-1, channels).astype(jnp.float32) + layer_scale * branch).astype(
        jnp.bfloat16
    )
    cot_live = jnp.where(inside[:, None, None], cotangent, jnp.zeros_like(cotangent)).reshape(
        -1, channels
    )
    upstream = (layer_scale * cot_live.astype(jnp.float32)).astype(jnp.bfloat16)
    sum_down = lax.dot_general(
        active, upstream, (((0,), (0,)), ((), ())), preferred_element_type=jnp.float32
    )
    back_active = lax.dot_general(
        upstream, full_down, (((1,), (1,)), ((), ())), preferred_element_type=jnp.float32
    )
    back_before = (back_active * smooth_slope(before)).astype(jnp.bfloat16)
    sum_up = lax.dot_general(
        normed, back_before, (((0,), (0,)), ((), ())), preferred_element_type=jnp.float32
    )
    back_normed = lax.dot_general(
        back_before, full_up, (((1,), (1,)), ((), ())), preferred_element_type=jnp.float32
    )
    back_unit = back_normed * norm_gain
    back_depth = scale_inv * (
        back_unit
        - jnp.mean(back_unit, axis=-1, keepdims=True)
        - standard * jnp.mean(back_unit * standard, axis=-1, keepdims=True)
    )
    back_depth = back_depth.astype(jnp.bfloat16).reshape(rows_max, tile_cols, channels)
    tap_list = []
    for row_off in range(kernel):
        for col_off in range(kernel):
            tap_list.append(
                jnp.sum(
                    framed[row_off : row_off + rows_max, col_off : col_off + tile_cols].astype(
                        jnp.float32
                    )
                    * back_depth.astype(jnp.float32),
                    axis=(0, 1),
                )
            )
    tap_list.extend([jnp.zeros_like(tap_list[0])] * (64 - kernel * kernel))
    tap_terms = jnp.stack(tap_list, axis=0).reshape(8, 8, channels)
    rscale = 1.0 / math.sqrt(BAND_MEAN * lax.axis_size("lat") * tile_cols * lax.axis_size("lon"))
    up_part, down_part, grad_depth, arrivals = sum_weights(
        sum_up, sum_down, tap_terms, halo_edges(back_depth, live_rows), rscale
    )
    grad_depth = grad_depth.reshape(64, channels)[: kernel * kernel]
    framed_back = framed_by(back_depth, arrivals, live_rows)
    spread = jnp.zeros((rows_max, tile_cols, channels), jnp.float32)
    for row_off in range(kernel):
        for col_off in range(kernel):
            spread = spread + framed_back[
                6 - row_off : 6 - row_off + rows_max, 6 - col_off : 6 - col_off + tile_cols
            ].astype(jnp.float32) * depth_weight[row_off, col_off].astype(jnp.float32)
    grad_local = (
        cotangent.astype(jnp.float32) + covered.astype(jnp.float32)[:, :, None] * spread
    ).astype(jnp.bfloat16)
    grad_in = jnp.where(inside[:, None, None], grad_local, jnp.zeros_like(grad_local))
    block_out = jnp.where(
        inside[:, None, None],
        result.reshape(rows_max, tile_cols, channels),
        jnp.zeros_like(feature),
    )
    return (block_out, grad_in, up_part, down_part, grad_depth.reshape(kernel, kernel, channels))


def solution(mesh):
    placed = (
        P("lat", "lon", None),
        P("lat", "lon"),
        P(),
        P(),
        P(),
        P(),
        P("lon", None),
        P(),
        P("lon", None),
        P(),
        P(),
        P("lat", "lon", None),
    )
    return jax.shard_map(
        shards,
        mesh=mesh,
        in_specs=placed,
        out_specs=(
            P("lat", "lon", None),
            P("lat", "lon", None),
            P("lon", None),
            P("lon", None),
            P(),
        ),
        check_vma=False,
    )
```

```python
import functools
import math

import jax
import jax.numpy as jnp
from jax import lax
from jax.experimental import pallas as pl
from jax.experimental.pallas import tpu as pltpu
from jax.sharding import PartitionSpec as P

BAND_MEAN = 16
TILE = 256


SQRT_TWO_PI = 0.7978845608028654
CUBIC = 0.044715
EPSILON = 1e-06


def places():
    lat, lon = lax.axis_index("lat"), lax.axis_index("lon")
    return lat, lon, lat // 4, (lat // 2) % 2, lat % 2, lon // 8, lon % 8


def remote(src, dst, sends, recvs, slot, device):
    return pltpu.make_async_remote_copy(
        src_ref=src,
        dst_ref=dst,
        send_sem=sends.at[slot],
        recv_sem=recvs.at[slot],
        device_id=device,
        device_id_type=pl.DeviceIdType.MESH,
    )


def greet(peers):
    barrier = pltpu.get_barrier_semaphore()
    for peer in peers:
        pl.semaphore_signal(barrier, inc=1, device_id=peer, device_id_type=pl.DeviceIdType.MESH)
    pl.semaphore_wait(barrier, len(peers))


def halo_peers(lat, lon):
    north, south = (lat + 15) % 16, (lat + 1) % 16
    west, east = (lon + 15) % 16, (lon + 1) % 16
    return [
        (lat, east), (lat, west), (south, lon), (north, lon),
        (south, east), (south, west), (north, east), (north, west),
    ]


def halo_copies(edges, arrivals, sends, recvs, base, peers):
    return [
        remote(edges[i], arrivals[i], sends, recvs, base + i, peers[i]) for i in range(8)
    ]


def halo_edges(field, live_rows):
    final = lax.dynamic_slice_in_dim(field, live_rows - 3, 3, 0)
    first = field[:3]
    return [
        field[:, -3:], field[:, :3], final, first,
        final[:, -3:], final[:, :3], first[:, -3:], first[:, :3],
    ]


def halo_shapes(rows, cols, channels):
    tall = jax.ShapeDtypeStruct((rows, 3, channels), jnp.bfloat16)
    wide = jax.ShapeDtypeStruct((3, cols, channels), jnp.bfloat16)
    corner = jax.ShapeDtypeStruct((3, 3, channels), jnp.bfloat16)
    return [tall, tall, wide, wide, corner, corner, corner, corner]


def framed_by(field, arrivals, live_rows):
    west, east, north, south, nw, ne, sw, se = arrivals
    lat = lax.axis_index("lat")
    above = jnp.concatenate([nw, north, ne], axis=1)
    below = jnp.concatenate([sw, south, se], axis=1)
    above = jnp.where(lat > 0, above, jnp.zeros_like(above))
    below = jnp.where(lat < lax.axis_size("lat") - 1, below, jnp.zeros_like(below))
    widened = jnp.concatenate([west, field, east], axis=1)
    stacked = jnp.concatenate([above, widened, jnp.zeros_like(above)], axis=0)
    return lax.dynamic_update_slice_in_dim(stacked, below, live_rows + 3, 0)


def gather_kernel(*refs):
    up_ref, down_ref = refs[:2]
    edges = refs[2:10]
    full_up, full_down = refs[10:12]
    arrivals = refs[12:20]
    sends, recvs = refs[20:]
    lat, lon, x, yh, c, yl, z = places()
    after = (lat, yl * 8 + (z + 1) % 8)
    ahead = (lat, yl * 8 + (z + 7) % 8)
    across = (lat, (1 - yl) * 8 + z)
    twin = (lat + 1 - 2 * c, lon)
    around = halo_peers(lat, lon)
    greet([after, ahead, across, twin] + around)
    started = []

    def parts(up, down, block, half):
        lanes = pl.ds(pl.multiple_of(half * 768, 768), 768)
        return (
            up.at[pl.ds(block * 3, 3), :, lanes],
            down.at[pl.ds(block * 12 + half * 6, 6)],
        )

    def copies(block, half, slot, device, own=False, which=(0, 1)):
        sources = parts(up_ref, down_ref, 0, half) if own else parts(full_up, full_down, block, half)
        targets = parts(full_up, full_down, block, half)
        return [
            remote(sources[i], targets[i], sends, recvs, slot * 2 + i, device) for i in which
        ]

    def mine(k):
        return yl * 8 + (z + 8 + k) % 8

    def theirs(k):
        return (1 - yl) * 8 + (z + 8 + k) % 8

    def send(block, slot, device, own=False, which=(0, 1)):
        for copy in copies(block, c, slot, device, own, which):
            copy.start()
            started.append(copy)

    def wait(block, slot, device, half=c, which=(0, 1)):
        for copy in copies(block, half, slot, device, False, which):
            copy.wait_recv()

    send(lon, 0, after, own=True)
    send(lon, 4, ahead, own=True)
    send(lon, 8, across, own=True)
    halos = halo_copies(edges, arrivals, sends, recvs, 64, around)
    for copy in halos:
        copy.start()
        started.append(copy)
    full_up[pl.ds(lon * 3, 3)] = up_ref[...]
    full_down[pl.ds(lon * 12, 12)] = down_ref[...]
    for k in (1, 2, 3):
        wait(mine(-k), k - 1, after)
        wait(mine(k), 3 + k, ahead)
        if k < 3:
            send(mine(-k), k, after)
            send(mine(k), 4 + k, ahead)
        else:
            send(mine(-3), 3, after, which=(0,))
            send(mine(3), 7, ahead, which=(1,))
        if k > 1:
            send(mine(-k), 7 + k, across)
            send(mine(k), 9 + k, across)
        send(mine(-k), 15 + k, twin)
        send(mine(k), 18 + k, twin)
        if k == 1:
            wait(theirs(0), 8, across)
            send(theirs(0), 14, after)
            send(theirs(0), 15, ahead)
            send(theirs(0), 23, twin)
    wait(theirs(-1), 14, after)
    wait(theirs(1), 15, ahead)
    send(theirs(-1), 24, twin)
    send(theirs(1), 25, twin)
    wait(mine(4), 3, after, which=(0,))
    wait(mine(4), 7, ahead, which=(1,))
    send(mine(4), 13, across)
    send(mine(4), 22, twin)
    for k in (2, 3):
        wait(theirs(-k), 7 + k, across)
        wait(theirs(k), 9 + k, across)
        send(theirs(-k), 24 + k, twin)
        send(theirs(k), 26 + k, twin)
    wait(theirs(4), 13, across)
    send(theirs(4), 30, twin)
    for k in (1, 2, 3):
        wait(mine(-k), 15 + k, twin, 1 - c)
        wait(mine(k), 18 + k, twin, 1 - c)
    wait(theirs(0), 23, twin, 1 - c)
    wait(theirs(-1), 24, twin, 1 - c)
    wait(theirs(1), 25, twin, 1 - c)
    wait(mine(4), 22, twin, 1 - c)
    for k in (2, 3):
        wait(theirs(-k), 24 + k, twin, 1 - c)
        wait(theirs(k), 26 + k, twin, 1 - c)
    wait(theirs(4), 30, twin, 1 - c)
    for copy in halos:
        copy.wait_recv()
    for copy in started:
        copy.wait_send()


def gather_weights(up_weight, down_weight, edges):
    vmem = pl.BlockSpec(memory_space=pltpu.VMEM)
    rows, cols, channels = edges[0].shape[0], edges[2].shape[1], edges[0].shape[2]
    full_up, full_down, *arrivals = pl.pallas_call(
        gather_kernel,
        out_shape=(
            jax.ShapeDtypeStruct((48, 8, 1536), jnp.bfloat16),
            jax.ShapeDtypeStruct((192, 8, 384), jnp.bfloat16),
            *halo_shapes(rows, cols, channels),
        ),
        in_specs=[vmem] * 10,
        out_specs=(vmem,) * 10,
        scratch_shapes=[pltpu.SemaphoreType.DMA((72,)), pltpu.SemaphoreType.DMA((72,))],
        compiler_params=pltpu.CompilerParams(collective_id=1, has_side_effects=True),
        name="gather_weights",
    )(up_weight.reshape(3, 8, 1536), down_weight.reshape(12, 8, 384), *edges)
    return full_up.reshape(384, 1536), full_down.reshape(1536, 384), arrivals


def sum_kernel(rscale, *refs):
    up_ref, down_ref, taps_ref = refs[:3]
    edges = refs[3:11]
    up_out, down_out, taps_out = refs[11:14]
    arrivals = refs[14:22]
    (
        twin_send, twin_recv, x_send, x_recv, d_send, d_recv, total, y_send, y_recv, z_send, z_recv,
        h_send, h_recv, pieces, others, tap_twin, tap_sum, tap_x, tap_ys, tap_yr, tap_z,
        tap_hs, tap_hr, sends, recvs,
    ) = refs[22:]
    lat, lon, x, yh, c, yl, z = places()
    f32, bf16 = jnp.float32, jnp.bfloat16
    twin = (lat + 1 - 2 * c, lon)
    column = [(((x + k) % 4) * 4 + yh * 2 + c, lon) for k in range(1, 4)]
    across = (lat, (1 - yl) * 8 + z)
    loop = [(lat, yl * 8 + (z + k) % 8) for k in range(1, 8)]
    far = (lat + 2 - 4 * yh, lon)
    around = halo_peers(lat, lon)
    greet([twin] + column + [across] + loop + [far] + around)
    started = []

    def launch(copy):
        copy.start()
        started.append(copy)
        return copy

    halos = [launch(copy) for copy in halo_copies(edges, arrivals, sends, recvs, 50, around)]
    tap_half = launch(
        remote(taps_ref.at[pl.ds((1 - c) * 4, 4)], tap_twin, sends, recvs, 22, twin)
    )
    order = (2, 1, 3, 0)

    def chunk_of(k):
        return (x + k) % 4

    def up_part(part):
        return up_ref[:, :, pl.ds(pl.multiple_of(part * 384, 384), 384)]

    twin_copies = {}
    for k in order:
        part = chunk_of(k)

        @pl.when(c == 1)
        def _():
            twin_send[k] = up_part(part).astype(bf16)

        @pl.when(c == 0)
        def _():
            @pl.loop(0, 16)
            def _(block):
                twin_send[k, pl.ds(block * 3, 3)] = down_ref[
                    pl.ds(block * 12 + part * 3, 3)
                ].astype(bf16)

        twin_copies[k] = launch(
            remote(twin_send.at[k], twin_recv.at[k], sends, recvs, k, twin)
        )
    upper, lower = pl.ds(0, 24), pl.ds(24, 24)
    for k in order:
        part = chunk_of(k)
        twin_copies[k].wait_recv()

        @pl.when(c == 0)
        def _():
            total[...] = up_part(part) + twin_recv[k].astype(f32)

        @pl.when(c == 1)
        def _():
            @pl.loop(0, 16)
            def _(block):
                total[pl.ds(block * 3, 3)] = down_ref[
                    pl.ds(block * 12 + part * 3, 3)
                ] + twin_recv[k, pl.ds(block * 3, 3)].astype(f32)

        if k == 2:
            d_send[...] = total[...].astype(bf16)
            via_next = launch(remote(d_send.at[upper], d_recv.at[0], sends, recvs, 20, column[0]))
            via_last = launch(remote(d_send.at[lower], d_recv.at[1], sends, recvs, 21, column[2]))
            tap_half.wait_recv()
            tap_sum[...] = taps_ref[pl.ds(c * 4, 4)] + tap_twin[...]
            for j in range(1, 4):
                launch(
                    remote(
                        tap_sum.at[(x + j) % 4], tap_x.at[j - 1], sends, recvs, 22 + j, column[j - 1]
                    )
                )
        elif k == 1:
            x_send[0, lower] = total[lower].astype(bf16)
            launch(remote(x_send.at[0, lower], x_recv.at[0, lower], sends, recvs, 4, column[0]))
            via_next.wait_recv()
            x_send[0, upper] = (total[upper] + d_recv[0].astype(f32)).astype(bf16)
            launch(remote(x_send.at[0, upper], x_recv.at[0, upper], sends, recvs, 5, column[0]))
        elif k == 3:
            x_send[1, upper] = total[upper].astype(bf16)
            launch(remote(x_send.at[1, upper], x_recv.at[1, upper], sends, recvs, 6, column[2]))
            via_last.wait_recv()
            x_send[1, lower] = (total[lower] + d_recv[1].astype(f32)).astype(bf16)
            launch(remote(x_send.at[1, lower], x_recv.at[1, lower], sends, recvs, 19, column[2]))
    for j in (1, 3, 2):
        remote(
            tap_sum.at[x], tap_x.at[j - 1], sends, recvs, 22 + j, column[j - 1]
        ).wait_recv()
    tap_ys[...] = (tap_sum[x] + tap_x[0]) + (tap_x[1] + tap_x[2])
    tap_y = launch(remote(tap_ys, tap_yr, sends, recvs, 26, across))
    tap_y.wait_recv()
    tap_z[z] = tap_ys[...] + tap_yr[...]
    for k in (4, 3, 5, 2, 6, 1, 7):
        launch(remote(tap_z.at[z], tap_z.at[z], sends, recvs, 26 + k, loop[k - 1]))
    remote(x_send.at[0, lower], x_recv.at[0, lower], sends, recvs, 4, column[0]).wait_recv()
    remote(x_send.at[0, upper], x_recv.at[0, upper], sends, recvs, 5, column[0]).wait_recv()
    remote(x_send.at[1, upper], x_recv.at[1, upper], sends, recvs, 6, column[2]).wait_recv()
    remote(x_send.at[1, lower], x_recv.at[1, lower], sends, recvs, 19, column[2]).wait_recv()
    far_half = pl.ds((1 - yl) * 24, 24)
    near_half = pl.ds(yl * 24, 24)

    def summed(rows):
        return total[rows] + (x_recv[0, rows].astype(f32) + x_recv[1, rows].astype(f32))

    y_send[...] = summed(far_half).astype(bf16)
    y_copy = launch(remote(y_send, y_recv, sends, recvs, 7, across))
    total[near_half] = summed(near_half)
    for k in (1, 7, 2, 6, 3, 5, 4):
        owner = (z + 8 - k) % 8
        remote(tap_z.at[owner], tap_z.at[owner], sends, recvs, 26 + k, loop[k - 1]).wait_recv()
    tap_hs[...] = ((tap_z[0] + tap_z[1]) + (tap_z[2] + tap_z[3])) + (
        (tap_z[4] + tap_z[5]) + (tap_z[6] + tap_z[7])
    )
    tap_h = launch(remote(tap_hs, tap_hr, sends, recvs, 34, far))
    y_copy.wait_recv()
    for k in (4, 3, 5, 2, 6, 1, 7):
        zk = (z + k) % 8
        z_send[k - 1] = (
            total[pl.ds(yl * 24 + zk * 3, 3)] + y_recv[pl.ds(zk * 3, 3)].astype(f32)
        ).astype(bf16)
        launch(remote(z_send.at[k - 1], z_recv.at[k - 1], sends, recvs, 7 + k, loop[k - 1]))
    piece = total[pl.ds(yl * 24 + z * 3, 3)] + y_recv[pl.ds(z * 3, 3)].astype(f32)
    tap_h.wait_recv()
    taps_out[c * 4 + x] = (tap_hs[...] + tap_hr[...]) * rscale
    for k in range(1, 4):
        launch(
            remote(
                taps_out.at[c * 4 + x], taps_out.at[c * 4 + x], sends, recvs, 34 + k, column[k - 1]
            )
        )
    for k in (1, 7, 2, 6, 3, 5, 4):
        remote(z_send.at[k - 1], z_recv.at[k - 1], sends, recvs, 7 + k, loop[k - 1]).wait_recv()
        piece = piece + z_recv[k - 1].astype(f32)
    h_send[...] = piece
    far_copy = launch(remote(h_send, h_recv, sends, recvs, 15, far))
    for k in range(1, 4):
        owner = c * 4 + (x + 4 - k) % 4
        remote(
            taps_out.at[owner], taps_out.at[owner], sends, recvs, 34 + k, column[k - 1]
        ).wait_recv()
    here, there = pl.ds(c * 4, 4), pl.ds((1 - c) * 4, 4)
    launch(remote(taps_out.at[here], taps_out.at[here], sends, recvs, 38, twin))
    far_copy.wait_recv()
    pieces[x] = (h_send[...] + h_recv[...]) * rscale
    for k in range(1, 4):
        launch(remote(pieces.at[x], pieces.at[x], sends, recvs, 15 + k, column[k - 1]))
    for k in range(1, 4):
        owner = (x + 4 - k) % 4
        remote(
            pieces.at[owner], pieces.at[owner], sends, recvs, 15 + k, column[k - 1]
        ).wait_recv()
    last = launch(remote(pieces, others, sends, recvs, 39, twin))
    remote(taps_out.at[there], taps_out.at[there], sends, recvs, 38, twin).wait_recv()
    for copy in halos:
        copy.wait_recv()
    last.wait_recv()

    def place(ups, downs):
        for part in range(4):
            up_out[:, :, part * 384 : part * 384 + 384] = ups[part]
            down_out[part * 3 : part * 3 + 3] = downs[part]

    @pl.when(c == 0)
    def _():
        place(pieces, others)

    @pl.when(c == 1)
    def _():
        place(others, pieces)

    for copy in started:
        copy.wait_send()


def sum_weights(sum_up, sum_down, taps, edges, rscale):
    vmem = pl.BlockSpec(memory_space=pltpu.VMEM)
    f32, bf16 = jnp.float32, jnp.bfloat16
    rows, cols, channels = edges[0].shape[0], edges[2].shape[1], edges[0].shape[2]
    up_part, down_part, taps, *arrivals = pl.pallas_call(
        functools.partial(sum_kernel, rscale),
        out_shape=(
            jax.ShapeDtypeStruct((3, 8, 1536), f32),
            jax.ShapeDtypeStruct((12, 8, 384), f32),
            jax.ShapeDtypeStruct((8, 8, 384), f32),
            *halo_shapes(rows, cols, channels),
        ),
        in_specs=[vmem] * 11,
        out_specs=(vmem,) * 11,
        scratch_shapes=[
            pltpu.VMEM((4, 48, 8, 384), bf16),
            pltpu.VMEM((4, 48, 8, 384), bf16),
            pltpu.VMEM((2, 48, 8, 384), bf16),
            pltpu.VMEM((2, 48, 8, 384), bf16),
            pltpu.VMEM((48, 8, 384), bf16),
            pltpu.VMEM((2, 24, 8, 384), bf16),
            pltpu.VMEM((48, 8, 384), f32),
            pltpu.VMEM((24, 8, 384), bf16),
            pltpu.VMEM((24, 8, 384), bf16),
            pltpu.VMEM((7, 3, 8, 384), bf16),
            pltpu.VMEM((7, 3, 8, 384), bf16),
            pltpu.VMEM((3, 8, 384), f32),
            pltpu.VMEM((3, 8, 384), f32),
            pltpu.VMEM((4, 3, 8, 384), f32),
            pltpu.VMEM((4, 3, 8, 384), f32),
            pltpu.VMEM((4, 8, 384), f32),
            pltpu.VMEM((4, 8, 384), f32),
            pltpu.VMEM((3, 8, 384), f32),
            pltpu.VMEM((8, 384), f32),
            pltpu.VMEM((8, 384), f32),
            pltpu.VMEM((8, 8, 384), f32),
            pltpu.VMEM((8, 384), f32),
            pltpu.VMEM((8, 384), f32),
            pltpu.SemaphoreType.DMA((58,)),
            pltpu.SemaphoreType.DMA((58,)),
        ],
        compiler_params=pltpu.CompilerParams(collective_id=2, has_side_effects=True),
        name="sum_weights",
    )(sum_up.reshape(48, 8, 1536), sum_down.reshape(192, 8, 384), taps, *edges)
    return up_part.reshape(24, 1536), down_part.reshape(96, 384), taps, arrivals


def token_kernel(
    live_ref, depth_ref, feature_ref, cot_ref, gain_ref, shift_ref, up_ref, up_bias_ref,
    down_ref, down_bias_ref, scale_ref, out_ref, back_ref, sum_up_ref, sum_down_ref,
):
    step = pl.program_id(0)
    f32, bf16 = jnp.float32, jnp.bfloat16
    rows = depth_ref.shape[0]

    def dot(left, right, dims):
        return lax.dot_general(left, right, ((dims[:1], dims[1:]), ((), ())), preferred_element_type=f32)

    @pl.when(step == 0)
    def _():
        sum_up_ref[...] = jnp.zeros_like(sum_up_ref)
        sum_down_ref[...] = jnp.zeros_like(sum_down_ref)

    index = step * rows + lax.broadcasted_iota(jnp.int32, (rows, 1), 0)
    inside = index < live_ref[0]
    depth = depth_ref[...]
    gain, layer_scale = gain_ref[...], scale_ref[...]
    offset = depth - jnp.mean(depth, axis=-1, keepdims=True)
    scale_inv = lax.rsqrt(jnp.mean(offset * offset, axis=-1, keepdims=True) + EPSILON)
    standard = offset * scale_inv
    normed = (standard * gain + shift_ref[...]).astype(bf16)
    upstream = jnp.where(inside, layer_scale * cot_ref[...].astype(f32), 0.0).astype(bf16)
    before = dot(normed, up_ref[...], (1, 0)) + up_bias_ref[...]
    square = before * before
    tangent = jnp.tanh(SQRT_TWO_PI * (before + CUBIC * square * before))
    half = 0.5 * (1.0 + tangent)
    active = (before * half).astype(bf16)
    slope = half + 0.5 * before * (1.0 - tangent * tangent) * SQRT_TWO_PI * (
        1.0 + 3.0 * CUBIC * square
    )
    back_active = dot(upstream, down_ref[...], (1, 1))
    back_before = (back_active * slope).astype(bf16)
    branch = dot(active, down_ref[...], (1, 0)) + down_bias_ref[...]
    result = feature_ref[...].astype(f32) + layer_scale * branch
    out_ref[...] = jnp.where(inside, result, 0.0).astype(bf16)
    back_unit = dot(back_before, up_ref[...], (1, 1)) * gain
    back_depth = scale_inv * (
        back_unit
        - jnp.mean(back_unit, axis=-1, keepdims=True)
        - standard * jnp.mean(back_unit * standard, axis=-1, keepdims=True)
    )
    back_ref[...] = back_depth.astype(bf16)
    sum_down_ref[...] += dot(active, upstream, (0, 0))
    sum_up_ref[...] += dot(normed, back_before, (0, 0))


def token_block(
    live, depth_rows, feature_rows, cot_rows, gain, shift, up, up_bias, down, down_bias, scale
):
    pixels, channels = depth_rows.shape
    hidden = up.shape[1]
    tile = TILE
    f32, bf16 = jnp.float32, jnp.bfloat16

    def per_tile():
        return pl.BlockSpec((tile, channels), lambda i: (i, 0))

    def whole(*shape):
        return pl.BlockSpec(shape, lambda i: (0, 0))

    return pl.pallas_call(
        token_kernel,
        grid=(pixels // tile,),
        out_shape=(
            jax.ShapeDtypeStruct((pixels, channels), bf16),
            jax.ShapeDtypeStruct((pixels, channels), bf16),
            jax.ShapeDtypeStruct((channels, hidden), f32),
            jax.ShapeDtypeStruct((hidden, channels), f32),
        ),
        in_specs=[
            pl.BlockSpec(memory_space=pltpu.SMEM),
            per_tile(),
            per_tile(),
            per_tile(),
            whole(1, channels),
            whole(1, channels),
            whole(channels, hidden),
            whole(1, hidden),
            whole(hidden, channels),
            whole(1, channels),
            whole(1, channels),
        ],
        out_specs=(per_tile(), per_tile(), whole(channels, hidden), whole(hidden, channels)),
        name="token_block",
    )(
        live, depth_rows, feature_rows, cot_rows, gain[None], shift[None], up, up_bias[None],
        down, down_bias[None], scale[None],
    )


def shards(
    feature,
    coverage,
    band_rows,
    depth_weight,
    norm_gain,
    norm_shift,
    up_weight,
    up_bias,
    down_weight,
    down_bias,
    layer_scale,
    cotangent,
):
    rows_max, tile_cols, channels = feature.shape
    kernel = depth_weight.shape[0]
    live_rows = lax.dynamic_index_in_dim(band_rows, lax.axis_index("lat"), 0, keepdims=False)
    inside = jnp.arange(rows_max, dtype=jnp.int32) < live_rows
    covered = jnp.where(inside[:, None], coverage, 0).astype(jnp.bfloat16)
    masked = feature * covered[:, :, None]
    full_up, full_down, arrivals = gather_weights(
        up_weight, down_weight, halo_edges(masked, live_rows)
    )
    framed = framed_by(masked, arrivals, live_rows)
    depth_out = jnp.zeros((rows_max, tile_cols, channels), jnp.float32)
    for row_off in range(kernel):
        for col_off in range(kernel):
            depth_out = depth_out + framed[
                row_off : row_off + rows_max, col_off : col_off + tile_cols
            ].astype(jnp.float32) * depth_weight[row_off, col_off].astype(jnp.float32)
    block_rows, back_rows, sum_up, sum_down = token_block(
        (live_rows * tile_cols).reshape(1),
        depth_out.reshape(-1, channels),
        feature.reshape(-1, channels),
        cotangent.reshape(-1, channels),
        norm_gain,
        norm_shift,
        full_up,
        up_bias,
        full_down,
        down_bias,
        layer_scale,
    )
    back_depth = back_rows.reshape(rows_max, tile_cols, channels)
    tap_list = []
    for row_off in range(kernel):
        for col_off in range(kernel):
            tap_list.append(
                jnp.sum(
                    framed[row_off : row_off + rows_max, col_off : col_off + tile_cols].astype(
                        jnp.float32
                    )
                    * back_depth.astype(jnp.float32),
                    axis=(0, 1),
                )
            )
    tap_list.extend([jnp.zeros_like(tap_list[0])] * (64 - kernel * kernel))
    tap_terms = jnp.stack(tap_list, axis=0).reshape(8, 8, channels)
    rscale = 1.0 / math.sqrt(BAND_MEAN * lax.axis_size("lat") * tile_cols * lax.axis_size("lon"))
    up_part, down_part, grad_depth, arrivals = sum_weights(
        sum_up, sum_down, tap_terms, halo_edges(back_depth, live_rows), rscale
    )
    grad_depth = grad_depth.reshape(64, channels)[: kernel * kernel]
    framed_back = framed_by(back_depth, arrivals, live_rows)
    spread = jnp.zeros((rows_max, tile_cols, channels), jnp.float32)
    for row_off in range(kernel):
        for col_off in range(kernel):
            spread = spread + framed_back[
                6 - row_off : 6 - row_off + rows_max, 6 - col_off : 6 - col_off + tile_cols
            ].astype(jnp.float32) * depth_weight[row_off, col_off].astype(jnp.float32)
    grad_local = (
        cotangent.astype(jnp.float32) + covered.astype(jnp.float32)[:, :, None] * spread
    ).astype(jnp.bfloat16)
    grad_in = jnp.where(inside[:, None, None], grad_local, jnp.zeros_like(grad_local))
    block_out = block_rows.reshape(rows_max, tile_cols, channels)
    return (block_out, grad_in, up_part, down_part, grad_depth.reshape(kernel, kernel, channels))


def solution(mesh):
    placed = (
        P("lat", "lon", None),
        P("lat", "lon"),
        P(),
        P(),
        P(),
        P(),
        P("lon", None),
        P(),
        P("lon", None),
        P(),
        P(),
        P("lat", "lon", None),
    )
    return jax.shard_map(
        shards,
        mesh=mesh,
        in_specs=placed,
        out_specs=(
            P("lat", "lon", None),
            P("lat", "lon", None),
            P("lon", None),
            P("lon", None),
            P(),
        ),
        check_vma=False,
    )
```

```python
import functools
import math

import jax
import jax.numpy as jnp
from jax import lax
from jax.experimental import pallas as pl
from jax.experimental.pallas import tpu as pltpu
from jax.sharding import PartitionSpec as P

BAND_MEAN = 16
TILE = 256


SQRT_TWO_PI = 0.7978845608028654
CUBIC = 0.044715
EPSILON = 1e-06


def places():
    lat, lon = lax.axis_index("lat"), lax.axis_index("lon")
    return lat, lon, lat // 4, (lat // 2) % 2, lat % 2, lon // 8, lon % 8


def remote(src, dst, sends, recvs, slot, device):
    return pltpu.make_async_remote_copy(
        src_ref=src,
        dst_ref=dst,
        send_sem=sends.at[slot],
        recv_sem=recvs.at[slot],
        device_id=device,
        device_id_type=pl.DeviceIdType.MESH,
    )


def greet(peers):
    barrier = pltpu.get_barrier_semaphore()
    for peer in peers:
        pl.semaphore_signal(barrier, inc=1, device_id=peer, device_id_type=pl.DeviceIdType.MESH)
    pl.semaphore_wait(barrier, len(peers))


def halo_peers(lat, lon):
    north, south = (lat + 15) % 16, (lat + 1) % 16
    west, east = (lon + 15) % 16, (lon + 1) % 16
    return [
        (lat, east), (lat, west), (south, lon), (north, lon),
        (south, east), (south, west), (north, east), (north, west),
    ]


def halo_copies(edges, arrivals, sends, recvs, base, peers):
    return [
        remote(edges[i], arrivals[i], sends, recvs, base + i, peers[i]) for i in range(8)
    ]


def halo_edges(field, live_rows):
    final = lax.dynamic_slice_in_dim(field, live_rows - 3, 3, 0)
    first = field[:3]
    return [
        field[:, -3:], field[:, :3], final, first,
        final[:, -3:], final[:, :3], first[:, -3:], first[:, :3],
    ]


def halo_shapes(rows, cols, channels):
    tall = jax.ShapeDtypeStruct((rows, 3, channels), jnp.bfloat16)
    wide = jax.ShapeDtypeStruct((3, cols, channels), jnp.bfloat16)
    corner = jax.ShapeDtypeStruct((3, 3, channels), jnp.bfloat16)
    return [tall, tall, wide, wide, corner, corner, corner, corner]


def framed_by(field, arrivals, live_rows):
    west, east, north, south, nw, ne, sw, se = arrivals
    lat = lax.axis_index("lat")
    above = jnp.concatenate([nw, north, ne], axis=1)
    below = jnp.concatenate([sw, south, se], axis=1)
    above = jnp.where(lat > 0, above, jnp.zeros_like(above))
    below = jnp.where(lat < lax.axis_size("lat") - 1, below, jnp.zeros_like(below))
    widened = jnp.concatenate([west, field, east], axis=1)
    stacked = jnp.concatenate([above, widened, jnp.zeros_like(above)], axis=0)
    return lax.dynamic_update_slice_in_dim(stacked, below, live_rows + 3, 0)


def gather_kernel(*refs):
    up_ref, down_ref = refs[:2]
    edges = refs[2:10]
    full_up, full_down = refs[10:12]
    arrivals = refs[12:20]
    sends, recvs = refs[20:]
    lat, lon, x, yh, c, yl, z = places()
    after = (lat, yl * 8 + (z + 1) % 8)
    ahead = (lat, yl * 8 + (z + 7) % 8)
    across = (lat, (1 - yl) * 8 + z)
    twin = (lat + 1 - 2 * c, lon)
    around = halo_peers(lat, lon)
    greet([after, ahead, across, twin] + around)
    started = []

    def parts(up, down, block, half):
        lanes = pl.ds(pl.multiple_of(half * 768, 768), 768)
        return (
            up.at[pl.ds(block * 3, 3), :, lanes],
            down.at[pl.ds(block * 12 + half * 6, 6)],
        )

    def copies(block, half, slot, device, own=False, which=(0, 1)):
        sources = parts(up_ref, down_ref, 0, half) if own else parts(full_up, full_down, block, half)
        targets = parts(full_up, full_down, block, half)
        return [
            remote(sources[i], targets[i], sends, recvs, slot * 2 + i, device) for i in which
        ]

    def mine(k):
        return yl * 8 + (z + 8 + k) % 8

    def theirs(k):
        return (1 - yl) * 8 + (z + 8 + k) % 8

    def send(block, slot, device, own=False, which=(0, 1)):
        for copy in copies(block, c, slot, device, own, which):
            copy.start()
            started.append(copy)

    def wait(block, slot, device, half=c, which=(0, 1)):
        for copy in copies(block, half, slot, device, False, which):
            copy.wait_recv()

    send(lon, 0, after, own=True)
    send(lon, 4, ahead, own=True)
    send(lon, 8, across, own=True)
    halos = halo_copies(edges, arrivals, sends, recvs, 64, around)
    for copy in halos:
        copy.start()
        started.append(copy)
    full_up[pl.ds(lon * 3, 3)] = up_ref[...]
    full_down[pl.ds(lon * 12, 12)] = down_ref[...]
    for k in (1, 2, 3):
        wait(mine(-k), k - 1, after)
        wait(mine(k), 3 + k, ahead)
        if k < 3:
            send(mine(-k), k, after)
            send(mine(k), 4 + k, ahead)
        else:
            send(mine(-3), 3, after, which=(0,))
            send(mine(3), 7, ahead, which=(1,))
        if k > 1:
            send(mine(-k), 7 + k, across)
            send(mine(k), 9 + k, across)
        send(mine(-k), 15 + k, twin)
        send(mine(k), 18 + k, twin)
        if k == 1:
            wait(theirs(0), 8, across)
            send(theirs(0), 14, after)
            send(theirs(0), 15, ahead)
            send(theirs(0), 23, twin)
    wait(theirs(-1), 14, after)
    wait(theirs(1), 15, ahead)
    send(theirs(-1), 24, twin)
    send(theirs(1), 25, twin)
    wait(mine(4), 3, after, which=(0,))
    wait(mine(4), 7, ahead, which=(1,))
    send(mine(4), 13, across)
    send(mine(4), 22, twin)
    for k in (2, 3):
        wait(theirs(-k), 7 + k, across)
        wait(theirs(k), 9 + k, across)
        send(theirs(-k), 24 + k, twin)
        send(theirs(k), 26 + k, twin)
    wait(theirs(4), 13, across)
    send(theirs(4), 30, twin)
    for k in (1, 2, 3):
        wait(mine(-k), 15 + k, twin, 1 - c)
        wait(mine(k), 18 + k, twin, 1 - c)
    wait(theirs(0), 23, twin, 1 - c)
    wait(theirs(-1), 24, twin, 1 - c)
    wait(theirs(1), 25, twin, 1 - c)
    wait(mine(4), 22, twin, 1 - c)
    for k in (2, 3):
        wait(theirs(-k), 24 + k, twin, 1 - c)
        wait(theirs(k), 26 + k, twin, 1 - c)
    wait(theirs(4), 30, twin, 1 - c)
    for copy in halos:
        copy.wait_recv()
    for copy in started:
        copy.wait_send()


def gather_weights(up_weight, down_weight, edges):
    vmem = pl.BlockSpec(memory_space=pltpu.VMEM)
    rows, cols, channels = edges[0].shape[0], edges[2].shape[1], edges[0].shape[2]
    full_up, full_down, *arrivals = pl.pallas_call(
        gather_kernel,
        out_shape=(
            jax.ShapeDtypeStruct((48, 8, 1536), jnp.bfloat16),
            jax.ShapeDtypeStruct((192, 8, 384), jnp.bfloat16),
            *halo_shapes(rows, cols, channels),
        ),
        in_specs=[vmem] * 10,
        out_specs=(vmem,) * 10,
        scratch_shapes=[pltpu.SemaphoreType.DMA((72,)), pltpu.SemaphoreType.DMA((72,))],
        compiler_params=pltpu.CompilerParams(collective_id=1, has_side_effects=True),
        name="gather_weights",
    )(up_weight.reshape(3, 8, 1536), down_weight.reshape(12, 8, 384), *edges)
    return full_up.reshape(384, 1536), full_down.reshape(1536, 384), arrivals


def tap_sums(framed_ref, back_ref, framed, shifted, back, taps_ref):
    f32 = jnp.float32

    @pl.loop(0, 38)
    def _(row):
        framed[row] = framed_ref[row].astype(f32)

    @pl.loop(0, 32)
    def _(row):
        back[row] = back_ref[row].astype(f32)

    taps_ref[6:8] = jnp.zeros((2, 8, 384), f32)
    for col_off in range(7):

        @pl.loop(0, 38)
        def _(row):
            shifted[row] = framed[row, col_off : col_off + 32]

        for group in range(3):
            lanes = slice(group * 128, group * 128 + 128)

            def add_row(row, sums):
                gradient = back[row, :, lanes]
                return tuple(
                    sums[off]
                    + jnp.sum((shifted[row + off, :, lanes] * gradient).reshape(4, 8, 128), axis=0)
                    for off in range(7)
                )

            sums = lax.fori_loop(0, 32, add_row, (jnp.zeros((8, 128), f32),) * 7)
            for off in range(7):
                tap = off * 7 + col_off
                taps_ref[tap // 8, tap % 8 : tap % 8 + 1, lanes] = jnp.sum(
                    sums[off], axis=0, keepdims=True
                )


def sum_kernel(rscale, *refs):
    up_ref, down_ref, framed_ref, back_ref = refs[:4]
    edges = refs[4:12]
    up_out, down_out, taps_out = refs[12:15]
    arrivals = refs[15:23]
    (
        twin_send, twin_recv, x_send, x_recv, d_send, d_recv, total, y_send, y_recv, z_send, z_recv,
        h_send, h_recv, pieces, others, tap_twin, tap_sum, tap_x, tap_ys, tap_yr, tap_z,
        tap_hs, tap_hr, taps_ref, framed, shifted, back, sends, recvs,
    ) = refs[23:]
    lat, lon, x, yh, c, yl, z = places()
    f32, bf16 = jnp.float32, jnp.bfloat16
    twin = (lat + 1 - 2 * c, lon)
    column = [(((x + k) % 4) * 4 + yh * 2 + c, lon) for k in range(1, 4)]
    across = (lat, (1 - yl) * 8 + z)
    loop = [(lat, yl * 8 + (z + k) % 8) for k in range(1, 8)]
    far = (lat + 2 - 4 * yh, lon)
    around = halo_peers(lat, lon)
    greet([twin] + column + [across] + loop + [far] + around)
    started = []

    def launch(copy):
        copy.start()
        started.append(copy)
        return copy

    halos = [launch(copy) for copy in halo_copies(edges, arrivals, sends, recvs, 50, around)]
    order = (2, 1, 3, 0)

    def chunk_of(k):
        return (x + k) % 4

    def up_part(part):
        return up_ref[:, :, pl.ds(pl.multiple_of(part * 384, 384), 384)]

    twin_copies = {}
    for k in order:
        part = chunk_of(k)

        @pl.when(c == 1)
        def _():
            twin_send[k] = up_part(part).astype(bf16)

        @pl.when(c == 0)
        def _():
            @pl.loop(0, 16)
            def _(block):
                twin_send[k, pl.ds(block * 3, 3)] = down_ref[
                    pl.ds(block * 12 + part * 3, 3)
                ].astype(bf16)

        twin_copies[k] = launch(
            remote(twin_send.at[k], twin_recv.at[k], sends, recvs, k, twin)
        )
    upper, lower = pl.ds(0, 24), pl.ds(24, 24)
    for k in order:
        part = chunk_of(k)
        twin_copies[k].wait_recv()

        @pl.when(c == 0)
        def _():
            total[...] = up_part(part) + twin_recv[k].astype(f32)

        @pl.when(c == 1)
        def _():
            @pl.loop(0, 16)
            def _(block):
                total[pl.ds(block * 3, 3)] = down_ref[
                    pl.ds(block * 12 + part * 3, 3)
                ] + twin_recv[k, pl.ds(block * 3, 3)].astype(f32)

        if k == 2:
            d_send[...] = total[...].astype(bf16)
            via_next = launch(remote(d_send.at[upper], d_recv.at[0], sends, recvs, 20, column[0]))
            via_last = launch(remote(d_send.at[lower], d_recv.at[1], sends, recvs, 21, column[2]))
        elif k == 1:
            x_send[0, lower] = total[lower].astype(bf16)
            launch(remote(x_send.at[0, lower], x_recv.at[0, lower], sends, recvs, 4, column[0]))
            via_next.wait_recv()
            x_send[0, upper] = (total[upper] + d_recv[0].astype(f32)).astype(bf16)
            launch(remote(x_send.at[0, upper], x_recv.at[0, upper], sends, recvs, 5, column[0]))
        elif k == 3:
            x_send[1, upper] = total[upper].astype(bf16)
            launch(remote(x_send.at[1, upper], x_recv.at[1, upper], sends, recvs, 6, column[2]))
            via_last.wait_recv()
            x_send[1, lower] = (total[lower] + d_recv[1].astype(f32)).astype(bf16)
            launch(remote(x_send.at[1, lower], x_recv.at[1, lower], sends, recvs, 19, column[2]))
    tap_sums(framed_ref, back_ref, framed, shifted, back, taps_ref)
    tap_half = launch(
        remote(taps_ref.at[pl.ds((1 - c) * 4, 4)], tap_twin, sends, recvs, 22, twin)
    )
    remote(x_send.at[0, lower], x_recv.at[0, lower], sends, recvs, 4, column[0]).wait_recv()
    remote(x_send.at[0, upper], x_recv.at[0, upper], sends, recvs, 5, column[0]).wait_recv()
    remote(x_send.at[1, upper], x_recv.at[1, upper], sends, recvs, 6, column[2]).wait_recv()
    remote(x_send.at[1, lower], x_recv.at[1, lower], sends, recvs, 19, column[2]).wait_recv()
    far_half = pl.ds((1 - yl) * 24, 24)
    near_half = pl.ds(yl * 24, 24)

    def summed(rows):
        return total[rows] + (x_recv[0, rows].astype(f32) + x_recv[1, rows].astype(f32))

    y_send[...] = summed(far_half).astype(bf16)
    y_copy = launch(remote(y_send, y_recv, sends, recvs, 7, across))
    tap_half.wait_recv()
    tap_sum[...] = taps_ref[pl.ds(c * 4, 4)] + tap_twin[...]
    for j in range(1, 4):
        launch(
            remote(tap_sum.at[(x + j) % 4], tap_x.at[j - 1], sends, recvs, 22 + j, column[j - 1])
        )
    total[near_half] = summed(near_half)
    y_copy.wait_recv()
    for k in (4, 3, 5, 2, 6, 1, 7):
        zk = (z + k) % 8
        z_send[k - 1] = (
            total[pl.ds(yl * 24 + zk * 3, 3)] + y_recv[pl.ds(zk * 3, 3)].astype(f32)
        ).astype(bf16)
        launch(remote(z_send.at[k - 1], z_recv.at[k - 1], sends, recvs, 7 + k, loop[k - 1]))
    piece = total[pl.ds(yl * 24 + z * 3, 3)] + y_recv[pl.ds(z * 3, 3)].astype(f32)
    for j in (1, 3, 2):
        remote(tap_sum.at[x], tap_x.at[j - 1], sends, recvs, 22 + j, column[j - 1]).wait_recv()
    tap_ys[...] = (tap_sum[x] + tap_x[0]) + (tap_x[1] + tap_x[2])
    tap_y = launch(remote(tap_ys, tap_yr, sends, recvs, 26, across))
    for k in (1, 7, 2, 6, 3, 5, 4):
        remote(z_send.at[k - 1], z_recv.at[k - 1], sends, recvs, 7 + k, loop[k - 1]).wait_recv()
        piece = piece + z_recv[k - 1].astype(f32)
    h_send[...] = piece
    far_copy = launch(remote(h_send, h_recv, sends, recvs, 15, far))
    tap_y.wait_recv()
    tap_z[z] = tap_ys[...] + tap_yr[...]
    for k in (4, 3, 5, 2, 6, 1, 7):
        launch(remote(tap_z.at[z], tap_z.at[z], sends, recvs, 26 + k, loop[k - 1]))
    far_copy.wait_recv()
    pieces[x] = (h_send[...] + h_recv[...]) * rscale
    for k in range(1, 4):
        launch(remote(pieces.at[x], pieces.at[x], sends, recvs, 15 + k, column[k - 1]))
    for k in (1, 7, 2, 6, 3, 5, 4):
        owner = (z + 8 - k) % 8
        remote(tap_z.at[owner], tap_z.at[owner], sends, recvs, 26 + k, loop[k - 1]).wait_recv()
    tap_hs[...] = ((tap_z[0] + tap_z[1]) + (tap_z[2] + tap_z[3])) + (
        (tap_z[4] + tap_z[5]) + (tap_z[6] + tap_z[7])
    )
    tap_h = launch(remote(tap_hs, tap_hr, sends, recvs, 34, far))
    for k in range(1, 4):
        owner = (x + 4 - k) % 4
        remote(
            pieces.at[owner], pieces.at[owner], sends, recvs, 15 + k, column[k - 1]
        ).wait_recv()
    last = launch(remote(pieces, others, sends, recvs, 39, twin))
    tap_h.wait_recv()
    taps_out[c * 4 + x] = (tap_hs[...] + tap_hr[...]) * rscale
    for k in range(1, 4):
        launch(
            remote(
                taps_out.at[c * 4 + x], taps_out.at[c * 4 + x], sends, recvs, 34 + k, column[k - 1]
            )
        )
    for k in range(1, 4):
        owner = c * 4 + (x + 4 - k) % 4
        remote(
            taps_out.at[owner], taps_out.at[owner], sends, recvs, 34 + k, column[k - 1]
        ).wait_recv()
    here, there = pl.ds(c * 4, 4), pl.ds((1 - c) * 4, 4)
    launch(remote(taps_out.at[here], taps_out.at[here], sends, recvs, 38, twin))
    last.wait_recv()

    def place(ups, downs):
        for part in range(4):
            up_out[:, :, part * 384 : part * 384 + 384] = ups[part]
            down_out[part * 3 : part * 3 + 3] = downs[part]

    @pl.when(c == 0)
    def _():
        place(pieces, others)

    @pl.when(c == 1)
    def _():
        place(others, pieces)

    for copy in halos:
        copy.wait_recv()
    remote(taps_out.at[there], taps_out.at[there], sends, recvs, 38, twin).wait_recv()
    for copy in started:
        copy.wait_send()


def sum_weights(sum_up, sum_down, framed, back_depth, edges, rscale):
    vmem = pl.BlockSpec(memory_space=pltpu.VMEM)
    f32, bf16 = jnp.float32, jnp.bfloat16
    rows, cols, channels = edges[0].shape[0], edges[2].shape[1], edges[0].shape[2]
    up_part, down_part, taps, *arrivals = pl.pallas_call(
        functools.partial(sum_kernel, rscale),
        out_shape=(
            jax.ShapeDtypeStruct((3, 8, 1536), f32),
            jax.ShapeDtypeStruct((12, 8, 384), f32),
            jax.ShapeDtypeStruct((8, 8, 384), f32),
            *halo_shapes(rows, cols, channels),
        ),
        in_specs=[vmem] * 12,
        out_specs=(vmem,) * 11,
        scratch_shapes=[
            pltpu.VMEM((4, 48, 8, 384), bf16),
            pltpu.VMEM((4, 48, 8, 384), bf16),
            pltpu.VMEM((2, 48, 8, 384), bf16),
            pltpu.VMEM((2, 48, 8, 384), bf16),
            pltpu.VMEM((48, 8, 384), bf16),
            pltpu.VMEM((2, 24, 8, 384), bf16),
            pltpu.VMEM((48, 8, 384), f32),
            pltpu.VMEM((24, 8, 384), bf16),
            pltpu.VMEM((24, 8, 384), bf16),
            pltpu.VMEM((7, 3, 8, 384), bf16),
            pltpu.VMEM((7, 3, 8, 384), bf16),
            pltpu.VMEM((3, 8, 384), f32),
            pltpu.VMEM((3, 8, 384), f32),
            pltpu.VMEM((4, 3, 8, 384), f32),
            pltpu.VMEM((4, 3, 8, 384), f32),
            pltpu.VMEM((4, 8, 384), f32),
            pltpu.VMEM((4, 8, 384), f32),
            pltpu.VMEM((3, 8, 384), f32),
            pltpu.VMEM((8, 384), f32),
            pltpu.VMEM((8, 384), f32),
            pltpu.VMEM((8, 8, 384), f32),
            pltpu.VMEM((8, 384), f32),
            pltpu.VMEM((8, 384), f32),
            pltpu.VMEM((8, 8, 384), f32),
            pltpu.VMEM((38, 38, 384), f32),
            pltpu.VMEM((38, 32, 384), f32),
            pltpu.VMEM((32, 32, 384), f32),
            pltpu.SemaphoreType.DMA((58,)),
            pltpu.SemaphoreType.DMA((58,)),
        ],
        compiler_params=pltpu.CompilerParams(collective_id=2, has_side_effects=True),
        name="sum_weights",
    )(sum_up.reshape(48, 8, 1536), sum_down.reshape(192, 8, 384), framed, back_depth, *edges)
    return up_part.reshape(24, 1536), down_part.reshape(96, 384), taps, arrivals


def token_kernel(
    live_ref, depth_ref, feature_ref, cot_ref, vector_ref, up_ref, up_bias_ref, down_ref,
    out_ref, back_ref, sum_up_ref, sum_down_ref,
):
    step = pl.program_id(0)
    f32, bf16 = jnp.float32, jnp.bfloat16
    rows = depth_ref.shape[0]

    def dot(left, right, dims):
        return lax.dot_general(left, right, ((dims[:1], dims[1:]), ((), ())), preferred_element_type=f32)

    @pl.when(step == 0)
    def _():
        sum_up_ref[...] = jnp.zeros_like(sum_up_ref)
        sum_down_ref[...] = jnp.zeros_like(sum_down_ref)

    index = step * rows + lax.broadcasted_iota(jnp.int32, (rows, 1), 0)
    inside = index < live_ref[0]
    depth = depth_ref[...]
    gain, shift, down_bias, layer_scale = (vector_ref[i : i + 1, :] for i in range(4))
    offset = depth - jnp.mean(depth, axis=-1, keepdims=True)
    scale_inv = lax.rsqrt(jnp.mean(offset * offset, axis=-1, keepdims=True) + EPSILON)
    standard = offset * scale_inv
    normed = (standard * gain + shift).astype(bf16)
    upstream = jnp.where(inside, layer_scale * cot_ref[...].astype(f32), 0.0).astype(bf16)
    before = dot(normed, up_ref[...], (1, 0)) + up_bias_ref[...]
    square = before * before
    tangent = jnp.tanh(SQRT_TWO_PI * (before + CUBIC * square * before))
    half = 0.5 * (1.0 + tangent)
    active = (before * half).astype(bf16)
    slope = half + 0.5 * before * (1.0 - tangent * tangent) * SQRT_TWO_PI * (
        1.0 + 3.0 * CUBIC * square
    )
    back_active = dot(upstream, down_ref[...], (1, 1))
    back_before = (back_active * slope).astype(bf16)
    branch = dot(active, down_ref[...], (1, 0)) + down_bias
    result = feature_ref[...].astype(f32) + layer_scale * branch
    out_ref[...] = jnp.where(inside, result, 0.0).astype(bf16)
    back_unit = dot(back_before, up_ref[...], (1, 1)) * gain
    back_depth = scale_inv * (
        back_unit
        - jnp.mean(back_unit, axis=-1, keepdims=True)
        - standard * jnp.mean(back_unit * standard, axis=-1, keepdims=True)
    )
    back_ref[...] = back_depth.astype(bf16)
    sum_down_ref[...] += dot(active, upstream, (0, 0))
    sum_up_ref[...] += dot(normed, back_before, (0, 0))


def token_block(
    live, depth_rows, feature_rows, cot_rows, gain, shift, up, up_bias, down, down_bias, scale
):
    pixels, channels = depth_rows.shape
    hidden = up.shape[1]
    tile = TILE
    f32, bf16 = jnp.float32, jnp.bfloat16

    def per_tile():
        return pl.BlockSpec((tile, channels), lambda i: (i, 0))

    def whole(*shape):
        return pl.BlockSpec(shape, lambda i: (0, 0))

    return pl.pallas_call(
        token_kernel,
        grid=(pixels // tile,),
        out_shape=(
            jax.ShapeDtypeStruct((pixels, channels), bf16),
            jax.ShapeDtypeStruct((pixels, channels), bf16),
            jax.ShapeDtypeStruct((channels, hidden), f32),
            jax.ShapeDtypeStruct((hidden, channels), f32),
        ),
        in_specs=[
            pl.BlockSpec(memory_space=pltpu.SMEM),
            per_tile(),
            per_tile(),
            per_tile(),
            whole(4, channels),
            whole(channels, hidden),
            whole(1, hidden),
            whole(hidden, channels),
        ],
        out_specs=(per_tile(), per_tile(), whole(channels, hidden), whole(hidden, channels)),
        name="token_block",
    )(
        live, depth_rows, feature_rows, cot_rows, jnp.stack([gain, shift, down_bias, scale]),
        up, up_bias[None], down,
    )


def shards(
    feature,
    coverage,
    band_rows,
    depth_weight,
    norm_gain,
    norm_shift,
    up_weight,
    up_bias,
    down_weight,
    down_bias,
    layer_scale,
    cotangent,
):
    rows_max, tile_cols, channels = feature.shape
    kernel = depth_weight.shape[0]
    live_rows = lax.dynamic_index_in_dim(band_rows, lax.axis_index("lat"), 0, keepdims=False)
    inside = jnp.arange(rows_max, dtype=jnp.int32) < live_rows
    covered = jnp.where(inside[:, None], coverage, 0).astype(jnp.bfloat16)
    masked = feature * covered[:, :, None]
    full_up, full_down, arrivals = gather_weights(
        up_weight, down_weight, halo_edges(masked, live_rows)
    )
    framed = framed_by(masked, arrivals, live_rows)
    depth_out = jnp.zeros((rows_max, tile_cols, channels), jnp.float32)
    for row_off in range(kernel):
        for col_off in range(kernel):
            depth_out = depth_out + framed[
                row_off : row_off + rows_max, col_off : col_off + tile_cols
            ].astype(jnp.float32) * depth_weight[row_off, col_off].astype(jnp.float32)
    block_rows, back_rows, sum_up, sum_down = token_block(
        (live_rows * tile_cols).reshape(1),
        depth_out.reshape(-1, channels),
        feature.reshape(-1, channels),
        cotangent.reshape(-1, channels),
        norm_gain,
        norm_shift,
        full_up,
        up_bias,
        full_down,
        down_bias,
        layer_scale,
    )
    back_depth = back_rows.reshape(rows_max, tile_cols, channels)
    rscale = 1.0 / math.sqrt(BAND_MEAN * lax.axis_size("lat") * tile_cols * lax.axis_size("lon"))
    up_part, down_part, grad_depth, arrivals = sum_weights(
        sum_up, sum_down, framed, back_depth, halo_edges(back_depth, live_rows), rscale
    )
    grad_depth = grad_depth.reshape(64, channels)[: kernel * kernel]
    framed_back = framed_by(back_depth, arrivals, live_rows)
    spread = jnp.zeros((rows_max, tile_cols, channels), jnp.float32)
    for row_off in range(kernel):
        for col_off in range(kernel):
            spread = spread + framed_back[
                6 - row_off : 6 - row_off + rows_max, 6 - col_off : 6 - col_off + tile_cols
            ].astype(jnp.float32) * depth_weight[row_off, col_off].astype(jnp.float32)
    grad_local = (
        cotangent.astype(jnp.float32) + covered.astype(jnp.float32)[:, :, None] * spread
    ).astype(jnp.bfloat16)
    grad_in = jnp.where(inside[:, None, None], grad_local, jnp.zeros_like(grad_local))
    block_out = block_rows.reshape(rows_max, tile_cols, channels)
    return (block_out, grad_in, up_part, down_part, grad_depth.reshape(kernel, kernel, channels))


def solution(mesh):
    placed = (
        P("lat", "lon", None),
        P("lat", "lon"),
        P(),
        P(),
        P(),
        P(),
        P("lon", None),
        P(),
        P("lon", None),
        P(),
        P(),
        P("lat", "lon", None),
    )
    return jax.shard_map(
        shards,
        mesh=mesh,
        in_specs=placed,
        out_specs=(
            P("lat", "lon", None),
            P("lat", "lon", None),
            P("lon", None),
            P("lon", None),
            P(),
        ),
        check_vma=False,
    )
```

```python
import functools
import math

import jax
import jax.numpy as jnp
from jax import lax
from jax.experimental import pallas as pl
from jax.experimental.pallas import tpu as pltpu
from jax.sharding import PartitionSpec as P

BAND_MEAN = 16
TILE = 256


SQRT_TWO_PI = 0.7978845608028654
CUBIC = 0.044715
EPSILON = 1e-06


def places():
    lat, lon = lax.axis_index("lat"), lax.axis_index("lon")
    return lat, lon, lat // 4, (lat // 2) % 2, lat % 2, lon // 8, lon % 8


def remote(src, dst, sends, recvs, slot, device):
    return pltpu.make_async_remote_copy(
        src_ref=src,
        dst_ref=dst,
        send_sem=sends.at[slot],
        recv_sem=recvs.at[slot],
        device_id=device,
        device_id_type=pl.DeviceIdType.MESH,
    )


def greet(peers):
    barrier = pltpu.get_barrier_semaphore()
    for peer in peers:
        pl.semaphore_signal(barrier, inc=1, device_id=peer, device_id_type=pl.DeviceIdType.MESH)
    pl.semaphore_wait(barrier, len(peers))


def halo_peers(lat, lon):
    north, south = (lat + 15) % 16, (lat + 1) % 16
    west, east = (lon + 15) % 16, (lon + 1) % 16
    return [
        (lat, east), (lat, west), (south, lon), (north, lon),
        (south, east), (south, west), (north, east), (north, west),
    ]


def halo_copies(edges, arrivals, sends, recvs, base, peers):
    return [
        remote(edges[i], arrivals[i], sends, recvs, base + i, peers[i]) for i in range(8)
    ]


def halo_edges(field, live_rows):
    final = lax.dynamic_slice_in_dim(field, live_rows - 3, 3, 0)
    first = field[:3]
    return [
        field[:, -3:], field[:, :3], final, first,
        final[:, -3:], final[:, :3], first[:, -3:], first[:, :3],
    ]


def halo_shapes(rows, cols, channels):
    tall = jax.ShapeDtypeStruct((rows, 3, channels), jnp.bfloat16)
    wide = jax.ShapeDtypeStruct((3, cols, channels), jnp.bfloat16)
    corner = jax.ShapeDtypeStruct((3, 3, channels), jnp.bfloat16)
    return [tall, tall, wide, wide, corner, corner, corner, corner]


def framed_by(field, arrivals, live_rows):
    west, east, north, south, nw, ne, sw, se = arrivals
    lat = lax.axis_index("lat")
    above = jnp.concatenate([nw, north, ne], axis=1)
    below = jnp.concatenate([sw, south, se], axis=1)
    above = jnp.where(lat > 0, above, jnp.zeros_like(above))
    below = jnp.where(lat < lax.axis_size("lat") - 1, below, jnp.zeros_like(below))
    widened = jnp.concatenate([west, field, east], axis=1)
    stacked = jnp.concatenate([above, widened, jnp.zeros_like(above)], axis=0)
    return lax.dynamic_update_slice_in_dim(stacked, below, live_rows + 3, 0)


def gather_kernel(*refs):
    up_ref, down_ref = refs[:2]
    edges = refs[2:10]
    full_up, full_down = refs[10:12]
    arrivals = refs[12:20]
    sends, recvs = refs[20:]
    lat, lon, x, yh, c, yl, z = places()
    after = (lat, yl * 8 + (z + 1) % 8)
    ahead = (lat, yl * 8 + (z + 7) % 8)
    across = (lat, (1 - yl) * 8 + z)
    twin = (lat + 1 - 2 * c, lon)
    around = halo_peers(lat, lon)
    greet([after, ahead, across, twin] + around)
    started = []

    def parts(up, down, block, half):
        lanes = pl.ds(pl.multiple_of(half * 768, 768), 768)
        return (
            up.at[pl.ds(block * 3, 3), :, lanes],
            down.at[pl.ds(block * 12 + half * 6, 6)],
        )

    def copies(block, half, slot, device, own=False, which=(0, 1)):
        sources = parts(up_ref, down_ref, 0, half) if own else parts(full_up, full_down, block, half)
        targets = parts(full_up, full_down, block, half)
        return [
            remote(sources[i], targets[i], sends, recvs, slot * 2 + i, device) for i in which
        ]

    def mine(k):
        return yl * 8 + (z + 8 + k) % 8

    def theirs(k):
        return (1 - yl) * 8 + (z + 8 + k) % 8

    def send(block, slot, device, own=False, which=(0, 1)):
        for copy in copies(block, c, slot, device, own, which):
            copy.start()
            started.append(copy)

    def wait(block, slot, device, half=c, which=(0, 1)):
        for copy in copies(block, half, slot, device, False, which):
            copy.wait_recv()

    send(lon, 0, after, own=True)
    send(lon, 4, ahead, own=True)
    send(lon, 8, across, own=True)
    halos = halo_copies(edges, arrivals, sends, recvs, 64, around)
    for copy in halos:
        copy.start()
        started.append(copy)
    full_up[pl.ds(lon * 3, 3)] = up_ref[...]
    full_down[pl.ds(lon * 12, 12)] = down_ref[...]
    for k in (1, 2, 3):
        wait(mine(-k), k - 1, after)
        wait(mine(k), 3 + k, ahead)
        if k < 3:
            send(mine(-k), k, after)
            send(mine(k), 4 + k, ahead)
        else:
            send(mine(-3), 3, after, which=(0,))
            send(mine(3), 7, ahead, which=(1,))
        if k > 1:
            send(mine(-k), 7 + k, across)
            send(mine(k), 9 + k, across)
        send(mine(-k), 15 + k, twin)
        send(mine(k), 18 + k, twin)
        if k == 1:
            wait(theirs(0), 8, across)
            send(theirs(0), 14, after)
            send(theirs(0), 15, ahead)
            send(theirs(0), 23, twin)
    wait(theirs(-1), 14, after)
    wait(theirs(1), 15, ahead)
    send(theirs(-1), 24, twin)
    send(theirs(1), 25, twin)
    wait(mine(4), 3, after, which=(0,))
    wait(mine(4), 7, ahead, which=(1,))
    send(mine(4), 13, across)
    send(mine(4), 22, twin)
    for k in (2, 3):
        wait(theirs(-k), 7 + k, across)
        wait(theirs(k), 9 + k, across)
        send(theirs(-k), 24 + k, twin)
        send(theirs(k), 26 + k, twin)
    wait(theirs(4), 13, across)
    send(theirs(4), 30, twin)
    for k in (1, 2, 3):
        wait(mine(-k), 15 + k, twin, 1 - c)
        wait(mine(k), 18 + k, twin, 1 - c)
    wait(theirs(0), 23, twin, 1 - c)
    wait(theirs(-1), 24, twin, 1 - c)
    wait(theirs(1), 25, twin, 1 - c)
    wait(mine(4), 22, twin, 1 - c)
    for k in (2, 3):
        wait(theirs(-k), 24 + k, twin, 1 - c)
        wait(theirs(k), 26 + k, twin, 1 - c)
    wait(theirs(4), 30, twin, 1 - c)
    for copy in halos:
        copy.wait_recv()
    for copy in started:
        copy.wait_send()


def gather_weights(up_weight, down_weight, edges):
    vmem = pl.BlockSpec(memory_space=pltpu.VMEM)
    rows, cols, channels = edges[0].shape[0], edges[2].shape[1], edges[0].shape[2]
    full_up, full_down, *arrivals = pl.pallas_call(
        gather_kernel,
        out_shape=(
            jax.ShapeDtypeStruct((48, 8, 1536), jnp.bfloat16),
            jax.ShapeDtypeStruct((192, 8, 384), jnp.bfloat16),
            *halo_shapes(rows, cols, channels),
        ),
        in_specs=[vmem] * 10,
        out_specs=(vmem,) * 10,
        scratch_shapes=[pltpu.SemaphoreType.DMA((72,)), pltpu.SemaphoreType.DMA((72,))],
        compiler_params=pltpu.CompilerParams(collective_id=1, has_side_effects=True),
        name="gather_weights",
    )(up_weight.reshape(3, 8, 1536), down_weight.reshape(12, 8, 384), *edges)
    return full_up.reshape(384, 1536), full_down.reshape(1536, 384), arrivals


def tap_sums(framed_ref, back_ref, framed, shifted, back, taps_ref):
    f32 = jnp.float32

    @pl.loop(0, 38)
    def _(row):
        framed[row] = framed_ref[row].astype(f32)

    @pl.loop(0, 32)
    def _(row):
        back[row] = back_ref[row].astype(f32)

    taps_ref[6:8] = jnp.zeros((2, 8, 384), f32)
    for col_off in range(7):

        @pl.loop(0, 38)
        def _(row):
            shifted[row] = framed[row, col_off : col_off + 32]

        for group in range(3):
            lanes = slice(group * 128, group * 128 + 128)

            def add_row(row, sums):
                gradient = back[row, :, lanes]
                return tuple(
                    sums[off]
                    + jnp.sum((shifted[row + off, :, lanes] * gradient).reshape(4, 8, 128), axis=0)
                    for off in range(7)
                )

            sums = lax.fori_loop(0, 32, add_row, (jnp.zeros((8, 128), f32),) * 7)
            for off in range(7):
                tap = off * 7 + col_off
                taps_ref[tap // 8, tap % 8 : tap % 8 + 1, lanes] = jnp.sum(
                    sums[off], axis=0, keepdims=True
                )


def sum_kernel(rscale, *refs):
    up_ref, down_ref, framed_ref, back_ref = refs[:4]
    edges = refs[4:12]
    up_out, down_out, taps_out = refs[12:15]
    arrivals = refs[15:23]
    (
        twin_send, twin_recv, x_send, x_recv, d_send, d_recv, total, y_send, y_recv, z_send, z_recv,
        h_send, h_recv, pieces, others, tap_twin, tap_sum, tap_x, tap_ys, tap_yr, tap_z,
        tap_hs, tap_hr, taps_ref, framed, shifted, back, sends, recvs,
    ) = refs[23:]
    lat, lon, x, yh, c, yl, z = places()
    f32, bf16 = jnp.float32, jnp.bfloat16
    twin = (lat + 1 - 2 * c, lon)
    column = [(((x + k) % 4) * 4 + yh * 2 + c, lon) for k in range(1, 4)]
    across = (lat, (1 - yl) * 8 + z)
    loop = [(lat, yl * 8 + (z + k) % 8) for k in range(1, 8)]
    far = (lat + 2 - 4 * yh, lon)
    around = halo_peers(lat, lon)
    greet([twin] + column + [across] + loop + [far] + around)
    started = []

    def launch(copy):
        copy.start()
        started.append(copy)
        return copy

    halos = [launch(copy) for copy in halo_copies(edges, arrivals, sends, recvs, 50, around)]
    order = (2, 1, 3, 0)

    def chunk_of(k):
        return (x + k) % 4

    def up_part(part):
        return up_ref[:, :, pl.ds(pl.multiple_of(part * 384, 384), 384)]

    twin_copies = {}
    for k in order:
        part = chunk_of(k)

        @pl.when(c == 1)
        def _():
            twin_send[k] = up_part(part).astype(bf16)

        @pl.when(c == 0)
        def _():
            @pl.loop(0, 16)
            def _(block):
                twin_send[k, pl.ds(block * 3, 3)] = down_ref[
                    pl.ds(block * 12 + part * 3, 3)
                ].astype(bf16)

        twin_copies[k] = launch(
            remote(twin_send.at[k], twin_recv.at[k], sends, recvs, k, twin)
        )
    upper, lower = pl.ds(0, 24), pl.ds(24, 24)
    for k in order:
        part = chunk_of(k)
        twin_copies[k].wait_recv()

        @pl.when(c == 0)
        def _():
            total[...] = up_part(part) + twin_recv[k].astype(f32)

        @pl.when(c == 1)
        def _():
            @pl.loop(0, 16)
            def _(block):
                total[pl.ds(block * 3, 3)] = down_ref[
                    pl.ds(block * 12 + part * 3, 3)
                ] + twin_recv[k, pl.ds(block * 3, 3)].astype(f32)

        if k == 2:
            d_send[...] = total[...].astype(bf16)
            via_next = launch(remote(d_send.at[upper], d_recv.at[0], sends, recvs, 20, column[0]))
            via_last = launch(remote(d_send.at[lower], d_recv.at[1], sends, recvs, 21, column[2]))
        elif k == 1:
            x_send[0, lower] = total[lower].astype(bf16)
            launch(remote(x_send.at[0, lower], x_recv.at[0, lower], sends, recvs, 4, column[0]))
            via_next.wait_recv()
            x_send[0, upper] = (total[upper] + d_recv[0].astype(f32)).astype(bf16)
            launch(remote(x_send.at[0, upper], x_recv.at[0, upper], sends, recvs, 5, column[0]))
        elif k == 3:
            x_send[1, upper] = total[upper].astype(bf16)
            launch(remote(x_send.at[1, upper], x_recv.at[1, upper], sends, recvs, 6, column[2]))
            via_last.wait_recv()
            x_send[1, lower] = (total[lower] + d_recv[1].astype(f32)).astype(bf16)
            launch(remote(x_send.at[1, lower], x_recv.at[1, lower], sends, recvs, 19, column[2]))
    tap_sums(framed_ref, back_ref, framed, shifted, back, taps_ref)
    tap_half = launch(
        remote(taps_ref.at[pl.ds((1 - c) * 4, 4)], tap_twin, sends, recvs, 22, twin)
    )
    remote(x_send.at[0, lower], x_recv.at[0, lower], sends, recvs, 4, column[0]).wait_recv()
    remote(x_send.at[0, upper], x_recv.at[0, upper], sends, recvs, 5, column[0]).wait_recv()
    remote(x_send.at[1, upper], x_recv.at[1, upper], sends, recvs, 6, column[2]).wait_recv()
    remote(x_send.at[1, lower], x_recv.at[1, lower], sends, recvs, 19, column[2]).wait_recv()
    far_half = pl.ds((1 - yl) * 24, 24)
    near_half = pl.ds(yl * 24, 24)

    def summed(rows):
        return total[rows] + (x_recv[0, rows].astype(f32) + x_recv[1, rows].astype(f32))

    y_send[...] = summed(far_half).astype(bf16)
    y_copy = launch(remote(y_send, y_recv, sends, recvs, 7, across))
    tap_half.wait_recv()
    tap_sum[...] = taps_ref[pl.ds(c * 4, 4)] + tap_twin[...]
    for j in range(1, 4):
        launch(
            remote(tap_sum.at[(x + j) % 4], tap_x.at[j - 1], sends, recvs, 22 + j, column[j - 1])
        )
    total[near_half] = summed(near_half)
    y_copy.wait_recv()
    for k in (4, 3, 5, 2, 6, 1, 7):
        zk = (z + k) % 8
        z_send[k - 1] = (
            total[pl.ds(yl * 24 + zk * 3, 3)] + y_recv[pl.ds(zk * 3, 3)].astype(f32)
        ).astype(bf16)
        launch(remote(z_send.at[k - 1], z_recv.at[k - 1], sends, recvs, 7 + k, loop[k - 1]))
    piece = total[pl.ds(yl * 24 + z * 3, 3)] + y_recv[pl.ds(z * 3, 3)].astype(f32)
    for j in (1, 3, 2):
        remote(tap_sum.at[x], tap_x.at[j - 1], sends, recvs, 22 + j, column[j - 1]).wait_recv()
    tap_ys[...] = (tap_sum[x] + tap_x[0]) + (tap_x[1] + tap_x[2])
    tap_y = launch(remote(tap_ys, tap_yr, sends, recvs, 26, across))
    for k in (1, 7, 2, 6, 3, 5, 4):
        remote(z_send.at[k - 1], z_recv.at[k - 1], sends, recvs, 7 + k, loop[k - 1]).wait_recv()
        piece = piece + z_recv[k - 1].astype(f32)
    h_send[...] = piece
    far_copy = launch(remote(h_send, h_recv, sends, recvs, 15, far))
    tap_y.wait_recv()
    tap_z[z] = tap_ys[...] + tap_yr[...]
    for k in (4, 3, 5, 2, 6, 1, 7):
        launch(remote(tap_z.at[z], tap_z.at[z], sends, recvs, 26 + k, loop[k - 1]))
    far_copy.wait_recv()
    pieces[x] = (h_send[...] + h_recv[...]) * rscale
    for k in range(1, 4):
        launch(remote(pieces.at[x], pieces.at[x], sends, recvs, 15 + k, column[k - 1]))
    for k in (1, 7, 2, 6, 3, 5, 4):
        owner = (z + 8 - k) % 8
        remote(tap_z.at[owner], tap_z.at[owner], sends, recvs, 26 + k, loop[k - 1]).wait_recv()
    tap_hs[...] = ((tap_z[0] + tap_z[1]) + (tap_z[2] + tap_z[3])) + (
        (tap_z[4] + tap_z[5]) + (tap_z[6] + tap_z[7])
    )
    tap_h = launch(remote(tap_hs, tap_hr, sends, recvs, 34, far))
    for k in range(1, 4):
        owner = (x + 4 - k) % 4
        remote(
            pieces.at[owner], pieces.at[owner], sends, recvs, 15 + k, column[k - 1]
        ).wait_recv()
    last = launch(remote(pieces, others, sends, recvs, 39, twin))
    tap_h.wait_recv()
    taps_out[c * 4 + x] = (tap_hs[...] + tap_hr[...]) * rscale
    for k in range(1, 4):
        launch(
            remote(
                taps_out.at[c * 4 + x], taps_out.at[c * 4 + x], sends, recvs, 34 + k, column[k - 1]
            )
        )
    for k in range(1, 4):
        owner = c * 4 + (x + 4 - k) % 4
        remote(
            taps_out.at[owner], taps_out.at[owner], sends, recvs, 34 + k, column[k - 1]
        ).wait_recv()
    here, there = pl.ds(c * 4, 4), pl.ds((1 - c) * 4, 4)
    launch(remote(taps_out.at[here], taps_out.at[here], sends, recvs, 38, twin))
    last.wait_recv()

    def place(ups, downs):
        for part in range(4):
            up_out[:, :, part * 384 : part * 384 + 384] = ups[part]
            down_out[part * 3 : part * 3 + 3] = downs[part]

    @pl.when(c == 0)
    def _():
        place(pieces, others)

    @pl.when(c == 1)
    def _():
        place(others, pieces)

    for copy in halos:
        copy.wait_recv()
    remote(taps_out.at[there], taps_out.at[there], sends, recvs, 38, twin).wait_recv()
    for copy in started:
        copy.wait_send()


def sum_weights(sum_up, sum_down, framed, back_depth, edges, rscale):
    vmem = pl.BlockSpec(memory_space=pltpu.VMEM)
    f32, bf16 = jnp.float32, jnp.bfloat16
    rows, cols, channels = edges[0].shape[0], edges[2].shape[1], edges[0].shape[2]
    up_part, down_part, taps, *arrivals = pl.pallas_call(
        functools.partial(sum_kernel, rscale),
        out_shape=(
            jax.ShapeDtypeStruct((3, 8, 1536), f32),
            jax.ShapeDtypeStruct((12, 8, 384), f32),
            jax.ShapeDtypeStruct((8, 8, 384), f32),
            *halo_shapes(rows, cols, channels),
        ),
        in_specs=[vmem] * 12,
        out_specs=(vmem,) * 11,
        scratch_shapes=[
            pltpu.VMEM((4, 48, 8, 384), bf16),
            pltpu.VMEM((4, 48, 8, 384), bf16),
            pltpu.VMEM((2, 48, 8, 384), bf16),
            pltpu.VMEM((2, 48, 8, 384), bf16),
            pltpu.VMEM((48, 8, 384), bf16),
            pltpu.VMEM((2, 24, 8, 384), bf16),
            pltpu.VMEM((48, 8, 384), f32),
            pltpu.VMEM((24, 8, 384), bf16),
            pltpu.VMEM((24, 8, 384), bf16),
            pltpu.VMEM((7, 3, 8, 384), bf16),
            pltpu.VMEM((7, 3, 8, 384), bf16),
            pltpu.VMEM((3, 8, 384), f32),
            pltpu.VMEM((3, 8, 384), f32),
            pltpu.VMEM((4, 3, 8, 384), f32),
            pltpu.VMEM((4, 3, 8, 384), f32),
            pltpu.VMEM((4, 8, 384), f32),
            pltpu.VMEM((4, 8, 384), f32),
            pltpu.VMEM((3, 8, 384), f32),
            pltpu.VMEM((8, 384), f32),
            pltpu.VMEM((8, 384), f32),
            pltpu.VMEM((8, 8, 384), f32),
            pltpu.VMEM((8, 384), f32),
            pltpu.VMEM((8, 384), f32),
            pltpu.VMEM((8, 8, 384), f32),
            pltpu.VMEM((38, 38, 384), f32),
            pltpu.VMEM((38, 32, 384), f32),
            pltpu.VMEM((32, 32, 384), f32),
            pltpu.SemaphoreType.DMA((58,)),
            pltpu.SemaphoreType.DMA((58,)),
        ],
        compiler_params=pltpu.CompilerParams(collective_id=2, has_side_effects=True),
        name="sum_weights",
    )(sum_up.reshape(48, 8, 1536), sum_down.reshape(192, 8, 384), framed, back_depth, *edges)
    return up_part.reshape(24, 1536), down_part.reshape(96, 384), taps, arrivals


def token_kernel(
    live_ref, depth_ref, feature_ref, cot_ref, vector_ref, up_ref, up_bias_ref, down_ref,
    out_ref, back_ref, sum_up_ref, sum_down_ref,
):
    step = pl.program_id(0)
    f32, bf16 = jnp.float32, jnp.bfloat16
    rows = depth_ref.shape[0]

    def dot(left, right, dims):
        return lax.dot_general(left, right, ((dims[:1], dims[1:]), ((), ())), preferred_element_type=f32)

    @pl.when(step == 0)
    def _():
        sum_up_ref[...] = jnp.zeros_like(sum_up_ref)
        sum_down_ref[...] = jnp.zeros_like(sum_down_ref)

    index = step * rows + lax.broadcasted_iota(jnp.int32, (rows, 1), 0)
    inside = index < live_ref[0]
    depth = depth_ref[...]
    gain, shift, down_bias, layer_scale = (vector_ref[i : i + 1, :] for i in range(4))
    offset = depth - jnp.mean(depth, axis=-1, keepdims=True)
    scale_inv = lax.rsqrt(jnp.mean(offset * offset, axis=-1, keepdims=True) + EPSILON)
    standard = offset * scale_inv
    normed = (standard * gain + shift).astype(bf16)
    upstream = jnp.where(inside, layer_scale * cot_ref[...].astype(f32), 0.0).astype(bf16)
    before = dot(normed, up_ref[...], (1, 0)) + up_bias_ref[...]
    square = before * before
    tangent = jnp.tanh(SQRT_TWO_PI * (before + CUBIC * square * before))
    half = 0.5 * (1.0 + tangent)
    active = (before * half).astype(bf16)
    slope = half + 0.5 * before * (1.0 - tangent * tangent) * SQRT_TWO_PI * (
        1.0 + 3.0 * CUBIC * square
    )
    back_active = dot(upstream, down_ref[...], (1, 1))
    back_before = (back_active * slope).astype(bf16)
    branch = dot(active, down_ref[...], (1, 0)) + down_bias
    result = feature_ref[...].astype(f32) + layer_scale * branch
    out_ref[...] = jnp.where(inside, result, 0.0).astype(bf16)
    back_unit = dot(back_before, up_ref[...], (1, 1)) * gain
    back_depth = scale_inv * (
        back_unit
        - jnp.mean(back_unit, axis=-1, keepdims=True)
        - standard * jnp.mean(back_unit * standard, axis=-1, keepdims=True)
    )
    back_ref[...] = back_depth.astype(bf16)
    sum_down_ref[...] += dot(active, upstream, (0, 0))
    sum_up_ref[...] += dot(normed, back_before, (0, 0))


def token_block(
    live, depth_rows, feature_rows, cot_rows, gain, shift, up, up_bias, down, down_bias, scale
):
    pixels, channels = depth_rows.shape
    hidden = up.shape[1]
    tile = TILE
    f32, bf16 = jnp.float32, jnp.bfloat16

    def per_tile():
        return pl.BlockSpec((tile, channels), lambda i: (i, 0))

    def whole(*shape):
        return pl.BlockSpec(shape, lambda i: (0, 0))

    return pl.pallas_call(
        token_kernel,
        grid=(pixels // tile,),
        out_shape=(
            jax.ShapeDtypeStruct((pixels, channels), bf16),
            jax.ShapeDtypeStruct((pixels, channels), bf16),
            jax.ShapeDtypeStruct((channels, hidden), f32),
            jax.ShapeDtypeStruct((hidden, channels), f32),
        ),
        in_specs=[
            pl.BlockSpec(memory_space=pltpu.SMEM),
            per_tile(),
            per_tile(),
            per_tile(),
            whole(4, channels),
            whole(channels, hidden),
            whole(1, hidden),
            whole(hidden, channels),
        ],
        out_specs=(per_tile(), per_tile(), whole(channels, hidden), whole(hidden, channels)),
        name="token_block",
    )(
        live, depth_rows, feature_rows, cot_rows, jnp.stack([gain, shift, down_bias, scale]),
        up, up_bias[None], down,
    )


def depthwise_kernel(framed_ref, weight_ref, out_ref, framed, shifted):
    f32 = jnp.float32

    @pl.loop(0, 38)
    def _(row):
        framed[row] = framed_ref[row].astype(f32)

    for col_off in range(7):

        @pl.loop(0, 38)
        def _(row):
            shifted[row] = framed[row, col_off : col_off + 32]

        for group in range(3):
            lanes = slice(group * 128, group * 128 + 128)
            taps = [
                jnp.broadcast_to(
                    weight_ref[off * 7 + col_off : off * 7 + col_off + 1, lanes], (8, 128)
                )[None]
                for off in range(7)
            ]

            @pl.loop(0, 16)
            def _(pair):
                rows = [
                    shifted[pair * 2 + off, :, lanes].reshape(4, 8, 128) for off in range(8)
                ]
                for side in range(2):
                    value = rows[side] * taps[0]
                    for off in range(1, 7):
                        value = value + rows[side + off] * taps[off]
                    value = value.reshape(32, 128)
                    if col_off:
                        value = value + out_ref[pair * 2 + side, :, lanes]
                    out_ref[pair * 2 + side, :, lanes] = value


def depthwise(framed, weights):
    vmem = pl.BlockSpec(memory_space=pltpu.VMEM)
    return pl.pallas_call(
        depthwise_kernel,
        out_shape=jax.ShapeDtypeStruct((32, 32, 384), jnp.float32),
        in_specs=[vmem, vmem],
        out_specs=vmem,
        scratch_shapes=[
            pltpu.VMEM((38, 38, 384), jnp.float32),
            pltpu.VMEM((38, 32, 384), jnp.float32),
        ],
        name="depthwise",
    )(framed, weights)


def shards(
    feature,
    coverage,
    band_rows,
    depth_weight,
    norm_gain,
    norm_shift,
    up_weight,
    up_bias,
    down_weight,
    down_bias,
    layer_scale,
    cotangent,
):
    rows_max, tile_cols, channels = feature.shape
    kernel = depth_weight.shape[0]
    live_rows = lax.dynamic_index_in_dim(band_rows, lax.axis_index("lat"), 0, keepdims=False)
    inside = jnp.arange(rows_max, dtype=jnp.int32) < live_rows
    covered = jnp.where(inside[:, None], coverage, 0).astype(jnp.bfloat16)
    masked = feature * covered[:, :, None]
    full_up, full_down, arrivals = gather_weights(
        up_weight, down_weight, halo_edges(masked, live_rows)
    )
    framed = framed_by(masked, arrivals, live_rows)
    weights = depth_weight.astype(jnp.float32).reshape(kernel * kernel, channels)
    depth_out = depthwise(framed, weights)
    block_rows, back_rows, sum_up, sum_down = token_block(
        (live_rows * tile_cols).reshape(1),
        depth_out.reshape(-1, channels),
        feature.reshape(-1, channels),
        cotangent.reshape(-1, channels),
        norm_gain,
        norm_shift,
        full_up,
        up_bias,
        full_down,
        down_bias,
        layer_scale,
    )
    back_depth = back_rows.reshape(rows_max, tile_cols, channels)
    rscale = 1.0 / math.sqrt(BAND_MEAN * lax.axis_size("lat") * tile_cols * lax.axis_size("lon"))
    up_part, down_part, grad_depth, arrivals = sum_weights(
        sum_up, sum_down, framed, back_depth, halo_edges(back_depth, live_rows), rscale
    )
    grad_depth = grad_depth.reshape(64, channels)[: kernel * kernel]
    framed_back = framed_by(back_depth, arrivals, live_rows)
    spread = depthwise(framed_back, weights[::-1])
    grad_local = (
        cotangent.astype(jnp.float32) + covered.astype(jnp.float32)[:, :, None] * spread
    ).astype(jnp.bfloat16)
    grad_in = jnp.where(inside[:, None, None], grad_local, jnp.zeros_like(grad_local))
    block_out = block_rows.reshape(rows_max, tile_cols, channels)
    return (block_out, grad_in, up_part, down_part, grad_depth.reshape(kernel, kernel, channels))


def solution(mesh):
    placed = (
        P("lat", "lon", None),
        P("lat", "lon"),
        P(),
        P(),
        P(),
        P(),
        P("lon", None),
        P(),
        P("lon", None),
        P(),
        P(),
        P("lat", "lon", None),
    )
    return jax.shard_map(
        shards,
        mesh=mesh,
        in_specs=placed,
        out_specs=(
            P("lat", "lon", None),
            P("lat", "lon", None),
            P("lon", None),
            P("lon", None),
            P(),
        ),
        check_vma=False,
    )
```

```python
import functools
import math

import jax
import jax.numpy as jnp
from jax import lax
from jax.experimental import pallas as pl
from jax.experimental.pallas import tpu as pltpu
from jax.sharding import PartitionSpec as P

BAND_MEAN = 16
TILE = 256


SQRT_TWO_PI = 0.7978845608028654
CUBIC = 0.044715
EPSILON = 1e-06


def places():
    lat, lon = lax.axis_index("lat"), lax.axis_index("lon")
    return lat, lon, lat // 4, (lat // 2) % 2, lat % 2, lon // 8, lon % 8


def remote(src, dst, sends, recvs, slot, device):
    return pltpu.make_async_remote_copy(
        src_ref=src,
        dst_ref=dst,
        send_sem=sends.at[slot],
        recv_sem=recvs.at[slot],
        device_id=device,
        device_id_type=pl.DeviceIdType.MESH,
    )


def greet(peers):
    barrier = pltpu.get_barrier_semaphore()
    for peer in peers:
        pl.semaphore_signal(barrier, inc=1, device_id=peer, device_id_type=pl.DeviceIdType.MESH)
    pl.semaphore_wait(barrier, len(peers))


def halo_peers(lat, lon):
    north, south = (lat + 15) % 16, (lat + 1) % 16
    west, east = (lon + 15) % 16, (lon + 1) % 16
    return [
        (lat, east), (lat, west), (south, lon), (north, lon),
        (south, east), (south, west), (north, east), (north, west),
    ]


def halo_copies(edges, arrivals, sends, recvs, base, peers):
    return [
        remote(edges[i], arrivals[i], sends, recvs, base + i, peers[i]) for i in range(8)
    ]


def halo_edges(field, live_rows):
    final = lax.dynamic_slice_in_dim(field, live_rows - 3, 3, 0)
    first = field[:3]
    return [
        field[:, -3:], field[:, :3], final, first,
        final[:, -3:], final[:, :3], first[:, -3:], first[:, :3],
    ]


def halo_shapes(rows, cols, channels):
    tall = jax.ShapeDtypeStruct((rows, 3, channels), jnp.bfloat16)
    wide = jax.ShapeDtypeStruct((3, cols, channels), jnp.bfloat16)
    corner = jax.ShapeDtypeStruct((3, 3, channels), jnp.bfloat16)
    return [tall, tall, wide, wide, corner, corner, corner, corner]


def framed_by(field, arrivals, live_rows):
    west, east, north, south, nw, ne, sw, se = arrivals
    lat = lax.axis_index("lat")
    above = jnp.concatenate([nw, north, ne], axis=1)
    below = jnp.concatenate([sw, south, se], axis=1)
    above = jnp.where(lat > 0, above, jnp.zeros_like(above))
    below = jnp.where(lat < lax.axis_size("lat") - 1, below, jnp.zeros_like(below))
    widened = jnp.concatenate([west, field, east], axis=1)
    stacked = jnp.concatenate([above, widened, jnp.zeros_like(above)], axis=0)
    return lax.dynamic_update_slice_in_dim(stacked, below, live_rows + 3, 0)


def gather_kernel(*refs):
    up_ref, down_ref = refs[:2]
    edges = refs[2:10]
    full_up, full_down = refs[10:12]
    arrivals = refs[12:20]
    sends, recvs = refs[20:]
    lat, lon, x, yh, c, yl, z = places()
    after = (lat, yl * 8 + (z + 1) % 8)
    ahead = (lat, yl * 8 + (z + 7) % 8)
    across = (lat, (1 - yl) * 8 + z)
    twin = (lat + 1 - 2 * c, lon)
    around = halo_peers(lat, lon)
    greet([after, ahead, across, twin] + around)
    started = []

    def parts(up, down, block, half):
        lanes = pl.ds(pl.multiple_of(half * 768, 768), 768)
        return (
            up.at[pl.ds(block * 3, 3), :, lanes],
            down.at[pl.ds(block * 12 + half * 6, 6)],
        )

    def copies(block, half, slot, device, own=False, which=(0, 1)):
        sources = parts(up_ref, down_ref, 0, half) if own else parts(full_up, full_down, block, half)
        targets = parts(full_up, full_down, block, half)
        return [
            remote(sources[i], targets[i], sends, recvs, slot * 2 + i, device) for i in which
        ]

    def mine(k):
        return yl * 8 + (z + 8 + k) % 8

    def theirs(k):
        return (1 - yl) * 8 + (z + 8 + k) % 8

    def send(block, slot, device, own=False, which=(0, 1)):
        for copy in copies(block, c, slot, device, own, which):
            copy.start()
            started.append(copy)

    def wait(block, slot, device, half=c, which=(0, 1)):
        for copy in copies(block, half, slot, device, False, which):
            copy.wait_recv()

    send(lon, 0, after, own=True)
    send(lon, 4, ahead, own=True)
    send(lon, 8, across, own=True)
    halos = halo_copies(edges, arrivals, sends, recvs, 64, around)
    for copy in halos:
        copy.start()
        started.append(copy)
    full_up[pl.ds(lon * 3, 3)] = up_ref[...]
    full_down[pl.ds(lon * 12, 12)] = down_ref[...]
    for k in (1, 2, 3):
        wait(mine(-k), k - 1, after)
        wait(mine(k), 3 + k, ahead)
        if k < 3:
            send(mine(-k), k, after)
            send(mine(k), 4 + k, ahead)
        else:
            send(mine(-3), 3, after, which=(0,))
            send(mine(3), 7, ahead, which=(1,))
        if k > 1:
            send(mine(-k), 7 + k, across)
            send(mine(k), 9 + k, across)
        send(mine(-k), 15 + k, twin)
        send(mine(k), 18 + k, twin)
        if k == 1:
            wait(theirs(0), 8, across)
            send(theirs(0), 14, after)
            send(theirs(0), 15, ahead)
            send(theirs(0), 23, twin)
    wait(theirs(-1), 14, after)
    wait(theirs(1), 15, ahead)
    send(theirs(-1), 24, twin)
    send(theirs(1), 25, twin)
    wait(mine(4), 3, after, which=(0,))
    wait(mine(4), 7, ahead, which=(1,))
    send(mine(4), 13, across)
    send(mine(4), 22, twin)
    for k in (2, 3):
        wait(theirs(-k), 7 + k, across)
        wait(theirs(k), 9 + k, across)
        send(theirs(-k), 24 + k, twin)
        send(theirs(k), 26 + k, twin)
    wait(theirs(4), 13, across)
    send(theirs(4), 30, twin)
    for k in (1, 2, 3):
        wait(mine(-k), 15 + k, twin, 1 - c)
        wait(mine(k), 18 + k, twin, 1 - c)
    wait(theirs(0), 23, twin, 1 - c)
    wait(theirs(-1), 24, twin, 1 - c)
    wait(theirs(1), 25, twin, 1 - c)
    wait(mine(4), 22, twin, 1 - c)
    for k in (2, 3):
        wait(theirs(-k), 24 + k, twin, 1 - c)
        wait(theirs(k), 26 + k, twin, 1 - c)
    wait(theirs(4), 30, twin, 1 - c)
    for copy in halos:
        copy.wait_recv()
    for copy in started:
        copy.wait_send()


def gather_weights(up_weight, down_weight, edges):
    vmem = pl.BlockSpec(memory_space=pltpu.VMEM)
    rows, cols, channels = edges[0].shape[0], edges[2].shape[1], edges[0].shape[2]
    full_up, full_down, *arrivals = pl.pallas_call(
        gather_kernel,
        out_shape=(
            jax.ShapeDtypeStruct((48, 8, 1536), jnp.bfloat16),
            jax.ShapeDtypeStruct((192, 8, 384), jnp.bfloat16),
            *halo_shapes(rows, cols, channels),
        ),
        in_specs=[vmem] * 10,
        out_specs=(vmem,) * 10,
        scratch_shapes=[pltpu.SemaphoreType.DMA((72,)), pltpu.SemaphoreType.DMA((72,))],
        compiler_params=pltpu.CompilerParams(collective_id=1, has_side_effects=True),
        name="gather_weights",
    )(up_weight.reshape(3, 8, 1536), down_weight.reshape(12, 8, 384), *edges)
    return full_up.reshape(384, 1536), full_down.reshape(1536, 384), arrivals


def tap_sums(framed_ref, back_ref, framed, shifted, back, taps_ref):
    f32 = jnp.float32

    @pl.loop(0, 38)
    def _(row):
        framed[row] = framed_ref[row].astype(f32)

    @pl.loop(0, 32)
    def _(row):
        back[row] = back_ref[row].astype(f32)

    taps_ref[6:8] = jnp.zeros((2, 8, 384), f32)
    for col_off in range(7):

        @pl.loop(0, 38)
        def _(row):
            shifted[row] = framed[row, col_off : col_off + 32]

        for group in range(3):
            lanes = slice(group * 128, group * 128 + 128)

            def add_row(row, sums):
                gradient = back[row, :, lanes]
                return tuple(
                    sums[off]
                    + jnp.sum((shifted[row + off, :, lanes] * gradient).reshape(4, 8, 128), axis=0)
                    for off in range(7)
                )

            sums = lax.fori_loop(0, 32, add_row, (jnp.zeros((8, 128), f32),) * 7)
            for off in range(7):
                tap = off * 7 + col_off
                taps_ref[tap // 8, tap % 8 : tap % 8 + 1, lanes] = jnp.sum(
                    sums[off], axis=0, keepdims=True
                )


def sum_kernel(rscale, *refs):
    up_ref, down_ref, framed_ref, back_ref = refs[:4]
    edges = refs[4:12]
    up_out, down_out, taps_out = refs[12:15]
    arrivals = refs[15:23]
    (
        twin_send, twin_recv, x_send, x_recv, d_send, d_recv, total, y_send, y_recv, z_send, z_recv,
        h_send, h_recv, pieces, others, tap_twin, tap_sum, tap_x, tap_ys, tap_yr, tap_z,
        tap_hs, tap_hr, taps_ref, framed, shifted, back, sends, recvs,
    ) = refs[23:]
    lat, lon, x, yh, c, yl, z = places()
    f32, bf16 = jnp.float32, jnp.bfloat16
    twin = (lat + 1 - 2 * c, lon)
    column = [(((x + k) % 4) * 4 + yh * 2 + c, lon) for k in range(1, 4)]
    across = (lat, (1 - yl) * 8 + z)
    loop = [(lat, yl * 8 + (z + k) % 8) for k in range(1, 8)]
    far = (lat + 2 - 4 * yh, lon)
    around = halo_peers(lat, lon)
    greet([twin] + column + [across] + loop + [far] + around)
    started = []

    def launch(copy):
        copy.start()
        started.append(copy)
        return copy

    halos = [launch(copy) for copy in halo_copies(edges, arrivals, sends, recvs, 50, around)]
    order = (2, 1, 3, 0)

    def chunk_of(k):
        return (x + k) % 4

    def up_part(part):
        return up_ref[:, :, pl.ds(pl.multiple_of(part * 384, 384), 384)]

    twin_copies = {}
    for k in order:
        part = chunk_of(k)

        @pl.when(c == 1)
        def _():
            twin_send[k] = up_part(part).astype(bf16)

        @pl.when(c == 0)
        def _():
            @pl.loop(0, 16)
            def _(block):
                twin_send[k, pl.ds(block * 3, 3)] = down_ref[
                    pl.ds(block * 12 + part * 3, 3)
                ].astype(bf16)

        twin_copies[k] = launch(
            remote(twin_send.at[k], twin_recv.at[k], sends, recvs, k, twin)
        )
    upper, lower = pl.ds(0, 24), pl.ds(24, 24)
    for k in order:
        part = chunk_of(k)
        twin_copies[k].wait_recv()

        @pl.when(c == 0)
        def _():
            total[...] = up_part(part) + twin_recv[k].astype(f32)

        @pl.when(c == 1)
        def _():
            @pl.loop(0, 16)
            def _(block):
                total[pl.ds(block * 3, 3)] = down_ref[
                    pl.ds(block * 12 + part * 3, 3)
                ] + twin_recv[k, pl.ds(block * 3, 3)].astype(f32)

        if k == 2:
            d_send[...] = total[...].astype(bf16)
            via_next = launch(remote(d_send.at[upper], d_recv.at[0], sends, recvs, 20, column[0]))
            via_last = launch(remote(d_send.at[lower], d_recv.at[1], sends, recvs, 21, column[2]))
        elif k == 1:
            x_send[0, lower] = total[lower].astype(bf16)
            launch(remote(x_send.at[0, lower], x_recv.at[0, lower], sends, recvs, 4, column[0]))
            via_next.wait_recv()
            x_send[0, upper] = (total[upper] + d_recv[0].astype(f32)).astype(bf16)
            launch(remote(x_send.at[0, upper], x_recv.at[0, upper], sends, recvs, 5, column[0]))
        elif k == 3:
            x_send[1, upper] = total[upper].astype(bf16)
            launch(remote(x_send.at[1, upper], x_recv.at[1, upper], sends, recvs, 6, column[2]))
            via_last.wait_recv()
            x_send[1, lower] = (total[lower] + d_recv[1].astype(f32)).astype(bf16)
            launch(remote(x_send.at[1, lower], x_recv.at[1, lower], sends, recvs, 19, column[2]))
    tap_sums(framed_ref, back_ref, framed, shifted, back, taps_ref)
    tap_half = launch(
        remote(taps_ref.at[pl.ds((1 - c) * 4, 4)], tap_twin, sends, recvs, 22, twin)
    )
    remote(x_send.at[0, lower], x_recv.at[0, lower], sends, recvs, 4, column[0]).wait_recv()
    remote(x_send.at[0, upper], x_recv.at[0, upper], sends, recvs, 5, column[0]).wait_recv()
    remote(x_send.at[1, upper], x_recv.at[1, upper], sends, recvs, 6, column[2]).wait_recv()
    remote(x_send.at[1, lower], x_recv.at[1, lower], sends, recvs, 19, column[2]).wait_recv()
    far_half = pl.ds((1 - yl) * 24, 24)
    near_half = pl.ds(yl * 24, 24)

    def summed(rows):
        return total[rows] + (x_recv[0, rows].astype(f32) + x_recv[1, rows].astype(f32))

    y_send[...] = summed(far_half).astype(bf16)
    y_copy = launch(remote(y_send, y_recv, sends, recvs, 7, across))
    tap_half.wait_recv()
    tap_sum[...] = taps_ref[pl.ds(c * 4, 4)] + tap_twin[...]
    for j in range(1, 4):
        launch(
            remote(tap_sum.at[(x + j) % 4], tap_x.at[j - 1], sends, recvs, 22 + j, column[j - 1])
        )
    total[near_half] = summed(near_half)
    y_copy.wait_recv()
    for k in (4, 3, 5, 2, 6, 1, 7):
        zk = (z + k) % 8
        z_send[k - 1] = (
            total[pl.ds(yl * 24 + zk * 3, 3)] + y_recv[pl.ds(zk * 3, 3)].astype(f32)
        ).astype(bf16)
        launch(remote(z_send.at[k - 1], z_recv.at[k - 1], sends, recvs, 7 + k, loop[k - 1]))
    piece = total[pl.ds(yl * 24 + z * 3, 3)] + y_recv[pl.ds(z * 3, 3)].astype(f32)
    for j in (1, 3, 2):
        remote(tap_sum.at[x], tap_x.at[j - 1], sends, recvs, 22 + j, column[j - 1]).wait_recv()
    tap_ys[...] = (tap_sum[x] + tap_x[0]) + (tap_x[1] + tap_x[2])
    tap_y = launch(remote(tap_ys, tap_yr, sends, recvs, 26, across))
    for k in (1, 7, 2, 6, 3, 5, 4):
        remote(z_send.at[k - 1], z_recv.at[k - 1], sends, recvs, 7 + k, loop[k - 1]).wait_recv()
        piece = piece + z_recv[k - 1].astype(f32)
    h_send[...] = piece
    far_copy = launch(remote(h_send, h_recv, sends, recvs, 15, far))
    tap_y.wait_recv()
    tap_z[z] = tap_ys[...] + tap_yr[...]
    for k in (4, 3, 5, 2, 6, 1, 7):
        launch(remote(tap_z.at[z], tap_z.at[z], sends, recvs, 26 + k, loop[k - 1]))
    far_copy.wait_recv()
    pieces[x] = (h_send[...] + h_recv[...]) * rscale
    for k in range(1, 4):
        launch(remote(pieces.at[x], pieces.at[x], sends, recvs, 15 + k, column[k - 1]))
    for k in (1, 7, 2, 6, 3, 5, 4):
        owner = (z + 8 - k) % 8
        remote(tap_z.at[owner], tap_z.at[owner], sends, recvs, 26 + k, loop[k - 1]).wait_recv()
    tap_hs[...] = ((tap_z[0] + tap_z[1]) + (tap_z[2] + tap_z[3])) + (
        (tap_z[4] + tap_z[5]) + (tap_z[6] + tap_z[7])
    )
    tap_h = launch(remote(tap_hs, tap_hr, sends, recvs, 34, far))
    for k in range(1, 4):
        owner = (x + 4 - k) % 4
        remote(
            pieces.at[owner], pieces.at[owner], sends, recvs, 15 + k, column[k - 1]
        ).wait_recv()
    last = launch(remote(pieces, others, sends, recvs, 39, twin))
    tap_h.wait_recv()
    taps_out[c * 4 + x] = (tap_hs[...] + tap_hr[...]) * rscale
    for k in range(1, 4):
        launch(
            remote(
                taps_out.at[c * 4 + x], taps_out.at[c * 4 + x], sends, recvs, 34 + k, column[k - 1]
            )
        )
    for k in range(1, 4):
        owner = c * 4 + (x + 4 - k) % 4
        remote(
            taps_out.at[owner], taps_out.at[owner], sends, recvs, 34 + k, column[k - 1]
        ).wait_recv()
    here, there = pl.ds(c * 4, 4), pl.ds((1 - c) * 4, 4)
    launch(remote(taps_out.at[here], taps_out.at[here], sends, recvs, 38, twin))
    last.wait_recv()

    def place(ups, downs):
        for part in range(4):
            up_out[:, :, part * 384 : part * 384 + 384] = ups[part]
            down_out[part * 3 : part * 3 + 3] = downs[part]

    @pl.when(c == 0)
    def _():
        place(pieces, others)

    @pl.when(c == 1)
    def _():
        place(others, pieces)

    for copy in halos:
        copy.wait_recv()
    remote(taps_out.at[there], taps_out.at[there], sends, recvs, 38, twin).wait_recv()
    for copy in started:
        copy.wait_send()


def sum_weights(sum_up, sum_down, framed, back_depth, edges, rscale):
    vmem = pl.BlockSpec(memory_space=pltpu.VMEM)
    f32, bf16 = jnp.float32, jnp.bfloat16
    rows, cols, channels = edges[0].shape[0], edges[2].shape[1], edges[0].shape[2]
    up_part, down_part, taps, *arrivals = pl.pallas_call(
        functools.partial(sum_kernel, rscale),
        out_shape=(
            jax.ShapeDtypeStruct((3, 8, 1536), f32),
            jax.ShapeDtypeStruct((12, 8, 384), f32),
            jax.ShapeDtypeStruct((8, 8, 384), f32),
            *halo_shapes(rows, cols, channels),
        ),
        in_specs=[vmem] * 12,
        out_specs=(vmem,) * 11,
        scratch_shapes=[
            pltpu.VMEM((4, 48, 8, 384), bf16),
            pltpu.VMEM((4, 48, 8, 384), bf16),
            pltpu.VMEM((2, 48, 8, 384), bf16),
            pltpu.VMEM((2, 48, 8, 384), bf16),
            pltpu.VMEM((48, 8, 384), bf16),
            pltpu.VMEM((2, 24, 8, 384), bf16),
            pltpu.VMEM((48, 8, 384), f32),
            pltpu.VMEM((24, 8, 384), bf16),
            pltpu.VMEM((24, 8, 384), bf16),
            pltpu.VMEM((7, 3, 8, 384), bf16),
            pltpu.VMEM((7, 3, 8, 384), bf16),
            pltpu.VMEM((3, 8, 384), f32),
            pltpu.VMEM((3, 8, 384), f32),
            pltpu.VMEM((4, 3, 8, 384), f32),
            pltpu.VMEM((4, 3, 8, 384), f32),
            pltpu.VMEM((4, 8, 384), f32),
            pltpu.VMEM((4, 8, 384), f32),
            pltpu.VMEM((3, 8, 384), f32),
            pltpu.VMEM((8, 384), f32),
            pltpu.VMEM((8, 384), f32),
            pltpu.VMEM((8, 8, 384), f32),
            pltpu.VMEM((8, 384), f32),
            pltpu.VMEM((8, 384), f32),
            pltpu.VMEM((8, 8, 384), f32),
            pltpu.VMEM((38, 38, 384), f32),
            pltpu.VMEM((38, 32, 384), f32),
            pltpu.VMEM((32, 32, 384), f32),
            pltpu.SemaphoreType.DMA((58,)),
            pltpu.SemaphoreType.DMA((58,)),
        ],
        compiler_params=pltpu.CompilerParams(collective_id=2, has_side_effects=True),
        name="sum_weights",
    )(sum_up.reshape(48, 8, 1536), sum_down.reshape(192, 8, 384), framed, back_depth, *edges)
    return up_part.reshape(24, 1536), down_part.reshape(96, 384), taps, arrivals


def token_kernel(
    live_ref, depth_ref, feature_ref, cot_ref, gain_ref, shift_ref, down_bias_ref, scale_ref, up_ref, up_bias_ref, down_ref,
    out_ref, back_ref, sum_up_ref, sum_down_ref,
):
    step = pl.program_id(0)
    f32, bf16 = jnp.float32, jnp.bfloat16
    rows = depth_ref.shape[0]

    def dot(left, right, dims):
        return lax.dot_general(left, right, ((dims[:1], dims[1:]), ((), ())), preferred_element_type=f32)

    @pl.when(step == 0)
    def _():
        sum_up_ref[...] = jnp.zeros_like(sum_up_ref)
        sum_down_ref[...] = jnp.zeros_like(sum_down_ref)

    index = step * rows + lax.broadcasted_iota(jnp.int32, (rows, 1), 0)
    inside = index < live_ref[0]
    depth = depth_ref[...]
    gain, shift, down_bias, layer_scale = (
        ref[...].reshape(1, -1) for ref in (gain_ref, shift_ref, down_bias_ref, scale_ref)
    )
    offset = depth - jnp.mean(depth, axis=-1, keepdims=True)
    scale_inv = lax.rsqrt(jnp.mean(offset * offset, axis=-1, keepdims=True) + EPSILON)
    standard = offset * scale_inv
    normed = (standard * gain + shift).astype(bf16)
    upstream = jnp.where(inside, layer_scale * cot_ref[...].astype(f32), 0.0).astype(bf16)
    before = dot(normed, up_ref[...], (1, 0)) + up_bias_ref[...].reshape(1, -1)
    square = before * before
    tangent = jnp.tanh(SQRT_TWO_PI * (before + CUBIC * square * before))
    half = 0.5 * (1.0 + tangent)
    active = (before * half).astype(bf16)
    slope = half + 0.5 * before * (1.0 - tangent * tangent) * SQRT_TWO_PI * (
        1.0 + 3.0 * CUBIC * square
    )
    back_active = dot(upstream, down_ref[...], (1, 1))
    back_before = (back_active * slope).astype(bf16)
    branch = dot(active, down_ref[...], (1, 0)) + down_bias
    result = feature_ref[...].astype(f32) + layer_scale * branch
    out_ref[...] = jnp.where(inside, result, 0.0).astype(bf16)
    back_unit = dot(back_before, up_ref[...], (1, 1)) * gain
    back_depth = scale_inv * (
        back_unit
        - jnp.mean(back_unit, axis=-1, keepdims=True)
        - standard * jnp.mean(back_unit * standard, axis=-1, keepdims=True)
    )
    back_ref[...] = back_depth.astype(bf16)
    sum_down_ref[...] += dot(active, upstream, (0, 0))
    sum_up_ref[...] += dot(normed, back_before, (0, 0))


def token_block(
    live, depth_rows, feature_rows, cot_rows, gain, shift, up, up_bias, down, down_bias, scale
):
    pixels, channels = depth_rows.shape
    hidden = up.shape[1]
    tile = TILE
    f32, bf16 = jnp.float32, jnp.bfloat16

    def per_tile():
        return pl.BlockSpec((tile, channels), lambda i: (i, 0))

    def whole(*shape):
        return pl.BlockSpec(shape, lambda i: (0, 0))

    return pl.pallas_call(
        token_kernel,
        grid=(pixels // tile,),
        out_shape=(
            jax.ShapeDtypeStruct((pixels, channels), bf16),
            jax.ShapeDtypeStruct((pixels, channels), bf16),
            jax.ShapeDtypeStruct((channels, hidden), f32),
            jax.ShapeDtypeStruct((hidden, channels), f32),
        ),
        in_specs=[
            pl.BlockSpec(memory_space=pltpu.SMEM),
            per_tile(),
            per_tile(),
            per_tile(),
            *[pl.BlockSpec((channels,), lambda i: (0,))] * 4,
            whole(channels, hidden),
            pl.BlockSpec((hidden,), lambda i: (0,)),
            whole(hidden, channels),
        ],
        out_specs=(per_tile(), per_tile(), whole(channels, hidden), whole(hidden, channels)),
        name="token_block",
    )(
        live, depth_rows, feature_rows, cot_rows, gain, shift, down_bias, scale, up, up_bias, down,
    )


def depthwise_kernel(flip, framed_ref, weight_ref, out_ref, framed, shifted):
    f32 = jnp.float32

    @pl.loop(0, 38)
    def _(row):
        framed[row] = framed_ref[row].astype(f32)

    for col_off in range(7):

        @pl.loop(0, 38)
        def _(row):
            shifted[row] = framed[row, col_off : col_off + 32]

        for group in range(3):
            lanes = slice(group * 128, group * 128 + 128)
            taps = [
                jnp.broadcast_to(
                    weight_ref[
                        6 - off if flip else off,
                        6 - col_off if flip else col_off : 7 - col_off if flip else col_off + 1,
                        lanes,
                    ].astype(f32),
                    (8, 128),
                )[None]
                for off in range(7)
            ]

            @pl.loop(0, 16)
            def _(pair):
                rows = [
                    shifted[pair * 2 + off, :, lanes].reshape(4, 8, 128) for off in range(8)
                ]
                for side in range(2):
                    value = rows[side] * taps[0]
                    for off in range(1, 7):
                        value = value + rows[side + off] * taps[off]
                    value = value.reshape(32, 128)
                    if col_off:
                        value = value + out_ref[pair * 2 + side, :, lanes]
                    out_ref[pair * 2 + side, :, lanes] = value


def depthwise(framed, weights, flip):
    vmem = pl.BlockSpec(memory_space=pltpu.VMEM)
    return pl.pallas_call(
        functools.partial(depthwise_kernel, flip),
        out_shape=jax.ShapeDtypeStruct((32, 32, 384), jnp.float32),
        in_specs=[vmem, vmem],
        out_specs=vmem,
        scratch_shapes=[
            pltpu.VMEM((38, 38, 384), jnp.float32),
            pltpu.VMEM((38, 32, 384), jnp.float32),
        ],
        name="depthwise",
    )(framed, weights)


def shards(
    feature,
    coverage,
    band_rows,
    depth_weight,
    norm_gain,
    norm_shift,
    up_weight,
    up_bias,
    down_weight,
    down_bias,
    layer_scale,
    cotangent,
):
    rows_max, tile_cols, channels = feature.shape
    kernel = depth_weight.shape[0]
    live_rows = lax.dynamic_index_in_dim(band_rows, lax.axis_index("lat"), 0, keepdims=False)
    inside = jnp.arange(rows_max, dtype=jnp.int32) < live_rows
    covered = jnp.where(inside[:, None], coverage, 0).astype(jnp.bfloat16)
    masked = feature * covered[:, :, None]
    full_up, full_down, arrivals = gather_weights(
        up_weight, down_weight, halo_edges(masked, live_rows)
    )
    framed = framed_by(masked, arrivals, live_rows)
    depth_out = depthwise(framed, depth_weight, False)
    block_rows, back_rows, sum_up, sum_down = token_block(
        (live_rows * tile_cols).reshape(1),
        depth_out.reshape(-1, channels),
        feature.reshape(-1, channels),
        cotangent.reshape(-1, channels),
        norm_gain,
        norm_shift,
        full_up,
        up_bias,
        full_down,
        down_bias,
        layer_scale,
    )
    back_depth = back_rows.reshape(rows_max, tile_cols, channels)
    rscale = 1.0 / math.sqrt(BAND_MEAN * lax.axis_size("lat") * tile_cols * lax.axis_size("lon"))
    up_part, down_part, grad_depth, arrivals = sum_weights(
        sum_up, sum_down, framed, back_depth, halo_edges(back_depth, live_rows), rscale
    )
    grad_depth = grad_depth.reshape(64, channels)[: kernel * kernel]
    framed_back = framed_by(back_depth, arrivals, live_rows)
    spread = depthwise(framed_back, depth_weight, True)
    grad_local = (
        cotangent.astype(jnp.float32) + covered.astype(jnp.float32)[:, :, None] * spread
    ).astype(jnp.bfloat16)
    grad_in = jnp.where(inside[:, None, None], grad_local, jnp.zeros_like(grad_local))
    block_out = block_rows.reshape(rows_max, tile_cols, channels)
    return (block_out, grad_in, up_part, down_part, grad_depth.reshape(kernel, kernel, channels))


def solution(mesh):
    placed = (
        P("lat", "lon", None),
        P("lat", "lon"),
        P(),
        P(),
        P(),
        P(),
        P("lon", None),
        P(),
        P("lon", None),
        P(),
        P(),
        P("lat", "lon", None),
    )
    return jax.shard_map(
        shards,
        mesh=mesh,
        in_specs=placed,
        out_specs=(
            P("lat", "lon", None),
            P("lat", "lon", None),
            P("lon", None),
            P("lon", None),
            P(),
        ),
        check_vma=False,
    )
```
